32 devices in a mesh: section: 2 (over y), row: 16 (over z, x, core).
Axes of the slice: x: 2, y: 2, z: 4, core: 2. Of those that a mesh axis runs over, the one named last changes fastest.
Arguments:
- pair: bfloat16 [2, 128, 128, 128], P(None, 'row'), may hold values from -6 to 6
- valid_tokens: int32 [2], replicated, may hold values from 32 to 128, as said below
- crop_order: int32 [2], replicated, may hold values from 0 to 1, each once
- w_proj: bfloat16 [2, 128, 384], P('section'), may hold values from -0.5 to 0.5
- w_out: bfloat16 [2, 64, 128], P('section'), may hold values from -0.75 to 0.75
- w_in: bfloat16 [2, 128, 1024], P('section'), may hold values from -0.5 to 0.5
- w_back: bfloat16 [2, 512, 128], P('section'), may hold values from -0.25 to 0.25
Outputs:
- final_pair: bfloat16 [2, 128, 128, 128], P('section', 'row')
The draws below stay inside these ranges and needn't reach their ends.
Inputs may be any that keep to these rules, and one draw needn't show every extreme that they name: `valid_tokens`: valid tokens of each crop; some crop is full and some other has 32. `crop_order`: each crop is taken at exactly one slot.
All inputs are finite; a program needn't handle non-finite values.
Results may differ from the reference program's by a relative error of at most 0.015.
Values may be sent and summed in bfloat16 or wider, within the bound.
No kernel may reach another device: no remote copies, remote signals or barrier semaphores. Data moves between devices by JAX's collectives and lax.ppermute only.
A program may use at most 64 MiB of HBM per device.

```python
import jax
import jax.numpy as jnp
from jax import lax

C = 128
CT = 64
TRANS = 512
CROP = 128
MICRO = 2
BLOCKS = 2


def draw_valid_tokens(key, part):
    base = jax.random.randint(key, (MICRO,), CROP // 4, CROP + 1)
    full_pick = jax.random.randint(jax.random.fold_in(key, 7), (), 0, MICRO)
    offset = jax.random.randint(jax.random.fold_in(key, 11), (), 1, MICRO)
    short_pick = (full_pick + offset) % MICRO
    slots = jnp.arange(MICRO)
    counts = jnp.where(slots == full_pick, CROP, base)
    counts = jnp.where(slots == short_pick, CROP // 4, counts)
    return counts.astype(jnp.int32)


def block_scale(rng, shape, split, smallest, top_value):
    def one(axis_at, blocks):
        draws = jax.random.uniform(jax.random.fold_in(jax.random.fold_in(rng, 6), axis_at), (blocks,), jnp.float32, smallest / len(split), top_value / len(split))
        return jnp.repeat(jnp.exp(draws), shape[axis_at] // blocks).reshape((-1,) + (1,) * (len(shape) - axis_at - 1))

    level = one(*split[0])
    for cut in split[1:]:
        level = level * one(*cut)
    return level


def gaussian(rng, shape, scale, reach, split=(), dtype=jnp.bfloat16):
    factor_of = block_scale(rng, shape, split, -0.22, 0.18) if split else 1.0
    result = jax.random.normal(rng, shape, jnp.float32) * scale * factor_of
    return jnp.minimum(jnp.maximum(result, -reach), reach).astype(dtype)


def setup_inputs(seed: int = 0) -> dict:
    streams_of = jax.random.split(jax.random.key(seed), 8)
    return {
        "pair": gaussian(streams_of[0], (MICRO, CROP, CROP, C), 1.0, 6.0, ((1, 16),)),
        "valid_tokens": draw_valid_tokens(jax.random.fold_in(streams_of[7], 71), 0),
        "crop_order": jax.random.permutation(streams_of[2], MICRO).astype(jnp.int32),
        "w_proj": gaussian(streams_of[3], (BLOCKS, C, 4 * CT + C), C ** -0.5, 0.5, ((0, 2),)),
        "w_out": gaussian(streams_of[4], (BLOCKS, CT, C), CT ** -0.5, 0.75, ((0, 2),)),
        "w_in": gaussian(streams_of[5], (BLOCKS, C, 2 * TRANS), C ** -0.5, 0.5, ((0, 2),)),
        "w_back": gaussian(streams_of[6], (BLOCKS, TRANS, C), TRANS ** -0.5, 0.25, ((0, 2),)),
    }


def layer_norm(value):
    mean = lax.optimization_barrier(jnp.mean(value, -1, keepdims=True))
    centred = value - mean
    var = lax.optimization_barrier(jnp.mean(centred * centred, -1, keepdims=True))
    return centred * lax.rsqrt(var + 1e-05)

def one_block(state, valid, w_proj, w_out, w_in, w_back):
    count = state.shape[0]
    width = state.shape[2]
    inner = w_out.shape[0]
    trans = w_back.shape[0]
    normed = layer_norm(state.astype(jnp.float32)).astype(jnp.bfloat16).reshape(count * count, width)
    proj = jnp.dot(normed, w_proj, preferred_element_type=jnp.float32).reshape(count, count, -1)
    keep = (jnp.arange(count) < valid).astype(jnp.float32)
    mask = keep[:, None, None] * keep[None, :, None]
    left = (mask * jax.nn.sigmoid(proj[..., inner:2 * inner]) * proj[..., :inner]).astype(jnp.bfloat16)
    right = (mask * jax.nn.sigmoid(proj[..., 3 * inner:4 * inner]) * proj[..., 2 * inner:3 * inner]).astype(jnp.bfloat16)
    gate = jax.nn.sigmoid(proj[..., 4 * inner:])
    tri = jnp.einsum('ikc,jkc->ijc', left.astype(jnp.float32), right.astype(jnp.float32), precision=lax.Precision.HIGHEST)
    tri_normed = layer_norm(tri).astype(jnp.bfloat16).reshape(count * count, inner)
    update = jnp.dot(tri_normed, w_out, preferred_element_type=jnp.float32).reshape(count, count, width)
    first = (state.astype(jnp.float32) + gate * update).astype(jnp.bfloat16)
    second = layer_norm(first.astype(jnp.float32)).astype(jnp.bfloat16).reshape(count * count, width)
    hidden = jnp.dot(second, w_in, preferred_element_type=jnp.float32)
    act = (jax.nn.silu(hidden[:, :trans]) * hidden[:, trans:]).astype(jnp.bfloat16)
    back = jnp.dot(act, w_back, preferred_element_type=jnp.float32).reshape(count, count, width)
    return (first.astype(jnp.float32) + back).astype(jnp.bfloat16)

def reference(pair, valid_tokens, crop_order, w_proj, w_out, w_in, w_back):
    results = []
    for slot in range(MICRO):
        crop = crop_order[slot]
        state = pair[crop]
        valid = valid_tokens[crop]
        for block in range(BLOCKS):
            state = one_block(state, valid, w_proj[block], w_out[block], w_in[block], w_back[block])
        results.append(state)
    return jnp.stack(results, 0)
```

```python
import functools

import jax
import jax.numpy as jnp
from jax import lax
from jax.experimental import pallas as pl
from jax.experimental.pallas import tpu as pltpu
from jax.sharding import PartitionSpec as P

F32 = jnp.float32
BF16 = jnp.bfloat16


def layer_norm(value, axis=-1):
    mean = jnp.mean(value, axis, keepdims=True)
    centred = value - mean
    var = jnp.mean(centred * centred, axis, keepdims=True)
    return centred * lax.rsqrt(var + 1e-05)


def fetch(condition, own, other, target, sem):
    @pl.when(condition)
    def _():
        pltpu.make_async_copy(own, target, sem).start()

    @pl.when(jnp.logical_not(condition))
    def _():
        pltpu.make_async_copy(other, target, sem).start()

    return pltpu.make_async_copy(own, target, sem)


def ordered_weights(weights, inner, share):
    wide = 2 * share
    row = lax.broadcasted_iota(jnp.int32, (4 * inner, 4 * inner), 0)
    column = lax.broadcasted_iota(jnp.int32, (4 * inner, 4 * inner), 1)
    gates, rest = lax.div(row, 2 * inner), lax.rem(row, 2 * inner)
    peer, slot = lax.div(rest, wide), lax.rem(rest, wide)
    side, channel = lax.div(slot, share), lax.rem(slot, share)
    source = side * (2 * inner) + gates * inner + peer * share + channel
    pick = jnp.where(column == source, 1.0, 0.0).astype(BF16)
    return lax.dot_general(
        pick, weights, (((1,), (1,)), ((), ())), preferred_element_type=F32
    ).astype(BF16)


def project(normed_ref, w_ref, valid, row_start, lr_ref, gate_ref, inner):
    peers, rows, wide, count = lr_ref.shape
    turned = ordered_weights(w_ref[:, : 4 * inner], inner, wide // 2)
    gate_w = w_ref[:, 4 * inner :]
    column = lax.broadcasted_iota(jnp.int32, (1, count), 1)
    for r in range(rows):
        normed = normed_ref[r * count : (r + 1) * count, :]
        proj = lax.dot_general(
            turned, normed, (((1,), (1,)), ((), ())), preferred_element_type=F32
        )
        keep = jnp.logical_and(column < valid, row_start + r < valid)
        mask = jnp.where(keep, 1.0, 0.0)
        sides = mask * jax.nn.sigmoid(proj[2 * inner :]) * proj[: 2 * inner]
        lr_ref[:, r] = sides.reshape(peers, wide, count).astype(BF16)
        gate_ref[r * count : (r + 1) * count, :] = jax.nn.sigmoid(
            jnp.dot(normed, gate_w, preferred_element_type=F32)
        )


def first_kernel(
    inner, order_ref, valid_ref, pair_ref, own_ref, other_ref, lr_ref, gate_ref, z_ref, w_ref, n_ref, sems
):
    section = lax.axis_index("section")
    rows, count = pair_ref.shape[1:3]
    row_start = lax.axis_index("row") * rows
    crop = order_ref[section]
    valid = valid_ref[crop]
    state = pltpu.make_async_copy(pair_ref.at[crop], z_ref, sems.at[0])
    state.start()
    weights = fetch(section == 0, own_ref.at[0], other_ref.at[0], w_ref, sems.at[1])
    state.wait()
    for r in range(rows):
        n_ref[r * count : (r + 1) * count, :] = layer_norm(z_ref[r].astype(F32)).astype(BF16)
    weights.wait()
    project(n_ref, w_ref, valid, row_start, lr_ref, gate_ref, inner)


def tri_kernel(in_ref, out_ref, wide_ref):
    peers, rows, wide, count = in_ref.shape
    share = wide // 2
    total = peers * rows
    wide_ref[...] = in_ref[...].astype(F32).reshape(total * wide, count)
    for c in range(share):
        left = wide_ref[pl.ds(c, total, stride=wide), :].astype(BF16)
        right = wide_ref[pl.ds(share + c, total, stride=wide), :].astype(BF16)
        tri = lax.dot_general(
            left, right, (((1,), (1,)), ((), ())), preferred_element_type=F32
        )
        out_ref[:, c] = tri.reshape(peers, rows, total).astype(BF16)


def update_kernel(
    block,
    blocks,
    inner,
    trans,
    order_ref,
    valid_ref,
    tri_ref,
    gate_ref,
    z_ref,
    own_ref,
    other_ref,
    wp_own_ref,
    wp_other_ref,
    *refs,
):
    last = block == blocks - 1
    if last:
        out_ref, t_ref, w_ref, n_ref, z1_ref, zs_ref, sems = refs
    else:
        out_ref, lr_ref, gate_out_ref, t_ref, w_ref, n_ref, z1_ref, zs_ref, sems, wp_ref = refs
    section = lax.axis_index("section")
    rows, count, width = out_ref.shape
    row_start = lax.axis_index("row") * rows
    crop = order_ref[section]
    valid = valid_ref[crop]
    if block == 0:
        state = pltpu.make_async_copy(z_ref.at[crop], zs_ref, sems.at[0])
    else:
        state = pltpu.make_async_copy(z_ref, zs_ref, sems.at[0])
    state.start()
    weights = fetch(section == block, own_ref, other_ref, w_ref, sems.at[1])
    if not last:
        following = fetch(
            section == block + 1, wp_own_ref.at[0], wp_other_ref.at[0], wp_ref, sems.at[2]
        )
    parts = width * (2 * trans // width)
    t_ref[...] = layer_norm(tri_ref[...].reshape(inner, rows, count).astype(F32), 0).reshape(
        inner * rows, count
    )
    weights.wait()
    state.wait()
    w_out = w_ref[parts + trans : parts + trans + inner, :]
    for r in range(rows):
        here = slice(r * count, (r + 1) * count)
        tri = t_ref[pl.ds(r, inner, stride=rows), :].astype(BF16)
        update = lax.dot_general(
            tri, w_out, (((0,), (0,)), ((), ())), preferred_element_type=F32
        )
        first = (zs_ref[r].astype(F32) + gate_ref[here, :] * update).astype(BF16)
        z1_ref[here, :] = first
        n_ref[here, :] = layer_norm(first.astype(F32)).astype(BF16)
    step = 2 * count
    for m in range(rows * count // step):
        here = slice(m * step, (m + 1) * step)
        normed = n_ref[here, :]
        total = z1_ref[here, :].astype(F32)
        for j in range(trans // width):
            gate_w = w_ref[j * width : (j + 1) * width, :]
            up_w = w_ref[trans + j * width : trans + (j + 1) * width, :]
            gate = jnp.dot(normed, gate_w, preferred_element_type=F32)
            up = jnp.dot(normed, up_w, preferred_element_type=F32)
            act = (jax.nn.silu(gate) * up).astype(BF16)
            back_w = w_ref[parts + j * width : parts + (j + 1) * width, :]
            total = total + jnp.dot(act, back_w, preferred_element_type=F32)
        done = total.astype(BF16)
        out_ref[2 * m : 2 * m + 2] = done.reshape(2, count, width)
        if not last:
            n_ref[here, :] = layer_norm(done.astype(F32)).astype(BF16)
    if not last:
        following.wait()
        project(n_ref, wp_ref, valid, row_start, lr_ref, gate_out_ref, inner)


def fast_body(pair, valid_tokens, crop_order, w_proj, w_out, w_in, w_back):
    crops, rows, count, width = pair.shape
    peers = lax.axis_size("row")
    inner, trans = w_out.shape[1], w_back.shape[1]
    share = inner // peers
    wide = 2 * share
    blocks = lax.axis_size("section")
    swap = [(0, 1), (1, 0)]
    rest = jnp.concatenate(
        [
            w_in[0].reshape(width, 2 * trans // width, width).transpose(1, 0, 2).reshape(2 * trans, width),
            w_back[0],
            w_out[0],
        ],
        0,
    )
    wp_other = lax.ppermute(w_proj, "section", swap)
    rest_other = lax.ppermute(rest, "section", swap)

    smem = pl.BlockSpec(memory_space=pltpu.SMEM)
    vmem = pl.BlockSpec(memory_space=pltpu.VMEM)
    anywhere = pl.BlockSpec(memory_space=pl.ANY)
    sides = jax.ShapeDtypeStruct((peers, rows, wide, count), BF16)
    gates = jax.ShapeDtypeStruct((rows * count, width), F32)
    state = jax.ShapeDtypeStruct((rows, count, width), BF16)

    lr, gate = pl.pallas_call(
        functools.partial(first_kernel, inner),
        out_shape=(sides, gates),
        in_specs=[smem, smem, anywhere, anywhere, anywhere],
        out_specs=(vmem, vmem),
        scratch_shapes=[
            pltpu.VMEM((rows, count, width), BF16),
            pltpu.VMEM(w_proj.shape[1:], BF16),
            pltpu.VMEM((rows * count, width), BF16),
            pltpu.SemaphoreType.DMA((2,)),
        ],
        name="project_first",
    )(crop_order, valid_tokens, pair, w_proj, wp_other)

    z = pair
    for block in range(blocks):
        last = block == blocks - 1
        whole = lax.all_to_all(lr, "row", split_axis=0, concat_axis=0, tiled=True)
        tri_part = pl.pallas_call(
            tri_kernel,
            out_shape=jax.ShapeDtypeStruct((peers, share, rows, count), BF16),
            in_specs=[vmem],
            out_specs=vmem,
            scratch_shapes=[pltpu.VMEM((peers * rows * wide, count), F32)],
            name="triangle",
        )(whole)
        tri = lax.all_to_all(tri_part, "row", split_axis=0, concat_axis=0, tiled=True)
        scratch = [
            pltpu.VMEM((inner * rows, count), F32),
            pltpu.VMEM(rest.shape, BF16),
            pltpu.VMEM((rows * count, width), BF16),
            pltpu.VMEM((rows * count, width), BF16),
            pltpu.VMEM((rows, count, width), BF16),
            pltpu.SemaphoreType.DMA((3,)),
        ]
        if not last:
            scratch.append(pltpu.VMEM(w_proj.shape[1:], BF16))
        result = pl.pallas_call(
            functools.partial(update_kernel, block, blocks, inner, trans),
            out_shape=(state,) if last else (state, sides, gates),
            in_specs=[smem, smem, vmem, vmem] + [anywhere] * 5,
            out_specs=(vmem,) if last else (vmem,) * 3,
            scratch_shapes=scratch,
            name="update_last" if last else "update",
        )(crop_order, valid_tokens, tri, gate, z, rest, rest_other, w_proj, wp_other)
        if last:
            (z,) = result
        else:
            z, lr, gate = result
    return z[None]


def pair_block(state, valid, row_start, w_proj, w_out, w_in, w_back):
    rows_here, count, width = state.shape
    inner, trans = w_out.shape[0], w_back.shape[0]
    normed = layer_norm(state.astype(F32)).astype(BF16).reshape(rows_here * count, width)
    proj = jnp.dot(normed, w_proj, preferred_element_type=F32).reshape(rows_here, count, -1)
    keep_cols = (jnp.arange(count) < valid).astype(F32)
    keep_rows = (row_start + jnp.arange(rows_here) < valid).astype(F32)
    mask = keep_rows[:, None, None] * keep_cols[None, :, None]
    left = (mask * jax.nn.sigmoid(proj[..., inner : 2 * inner]) * proj[..., :inner]).astype(BF16)
    right = (
        mask * jax.nn.sigmoid(proj[..., 3 * inner : 4 * inner]) * proj[..., 2 * inner : 3 * inner]
    ).astype(BF16)
    gate = jax.nn.sigmoid(proj[..., 4 * inner :])
    left_whole = lax.all_to_all(left, "row", split_axis=2, concat_axis=0, tiled=True)
    right_whole = lax.all_to_all(right, "row", split_axis=2, concat_axis=0, tiled=True)
    tri_part = jnp.einsum("ikc,jkc->ijc", left_whole, right_whole, preferred_element_type=F32)
    tri = lax.all_to_all(
        tri_part.astype(BF16), "row", split_axis=0, concat_axis=2, tiled=True
    ).astype(F32)
    tri_normed = layer_norm(tri).astype(BF16).reshape(rows_here * count, inner)
    update = jnp.dot(tri_normed, w_out, preferred_element_type=F32).reshape(rows_here, count, width)
    first = (state.astype(F32) + gate * update).astype(BF16)
    second = layer_norm(first.astype(F32)).astype(BF16).reshape(rows_here * count, width)
    hidden = jnp.dot(second, w_in, preferred_element_type=F32)
    act = (jax.nn.silu(hidden[:, :trans]) * hidden[:, trans:]).astype(BF16)
    back = jnp.dot(act, w_back, preferred_element_type=F32).reshape(rows_here, count, width)
    return (first.astype(F32) + back).astype(BF16)


def general_body(pair, valid_tokens, crop_order, w_proj, w_out, w_in, w_back):
    crops, rows_here = pair.shape[:2]
    row_start = lax.axis_index("row") * rows_here
    share = crops // lax.axis_size("section")
    section = lax.axis_index("section")
    weights = [
        lax.all_gather(w, "section", axis=0, tiled=True) for w in (w_proj, w_out, w_in, w_back)
    ]
    blocks = weights[0].shape[0]

    def one_crop(index, outputs):
        crop = crop_order[section * share + index]
        valid = valid_tokens[crop]
        state = lax.dynamic_index_in_dim(pair, crop, 0, keepdims=False)

        def apply_block(block, value):
            return pair_block(value, valid, row_start, *[w[block] for w in weights])

        final = lax.fori_loop(0, blocks, apply_block, state)
        return lax.dynamic_update_index_in_dim(outputs, final, index, 0)

    empty = jnp.zeros((share,) + pair.shape[1:], BF16)
    return lax.fori_loop(0, share, one_crop, empty)


def solution(mesh):
    sections, peers = mesh.shape["section"], mesh.shape["row"]

    def body(pair, valid_tokens, crop_order, w_proj, w_out, w_in, w_back):
        crops, rows, count, width = pair.shape
        inner, trans = w_out.shape[1], w_back.shape[1]
        fits = (
            sections == 2
            and crops == sections
            and w_proj.shape[0] == 1
            and rows == 8
            and count == width == 128
            and inner == 4 * peers
            and trans % width == 0
        )
        run = fast_body if fits else general_body
        return run(pair, valid_tokens, crop_order, w_proj, w_out, w_in, w_back)

    weights = P("section", None, None)
    return jax.shard_map(
        body,
        mesh=mesh,
        in_specs=(P(None, "row", None, None), P(), P(), weights, weights, weights, weights),
        out_specs=P("section", "row", None, None),
        check_vma=False,
    )
```

```python
import functools

import jax
import jax.numpy as jnp
from jax import lax
from jax.experimental import pallas as pl
from jax.experimental.pallas import tpu as pltpu
from jax.sharding import PartitionSpec as P

F32 = jnp.float32
BF16 = jnp.bfloat16
LIMIT = pltpu.CompilerParams(vmem_limit_bytes=16 * 2**20)


def layer_norm(value, axis=-1):
    mean = jnp.mean(value, axis, keepdims=True)
    centred = value - mean
    var = jnp.mean(centred * centred, axis, keepdims=True)
    return centred * lax.rsqrt(var + 1e-05)


def fetch(condition, own, other, target, sem):
    @pl.when(condition)
    def _():
        pltpu.make_async_copy(own, target, sem).start()

    @pl.when(jnp.logical_not(condition))
    def _():
        pltpu.make_async_copy(other, target, sem).start()

    return pltpu.make_async_copy(own, target, sem)


def ordered_weights(weights, inner, share):
    wide = 2 * share
    row = lax.broadcasted_iota(jnp.int32, (4 * inner, 4 * inner), 0)
    column = lax.broadcasted_iota(jnp.int32, (4 * inner, 4 * inner), 1)
    gates, rest = lax.div(row, 2 * inner), lax.rem(row, 2 * inner)
    peer, slot = lax.div(rest, wide), lax.rem(rest, wide)
    side, channel = lax.div(slot, share), lax.rem(slot, share)
    source = side * (2 * inner) + gates * inner + peer * share + channel
    pick = jnp.where(column == source, 1.0, 0.0).astype(BF16)
    return lax.dot_general(
        pick, weights, (((1,), (1,)), ((), ())), preferred_element_type=F32
    ).astype(BF16)


def project(normed_ref, w_ref, keep_ref, lr_ref, inner):
    peers, rows, wide, count = lr_ref.shape
    turned = ordered_weights(w_ref[:, : 4 * inner], inner, wide // 2)
    for r in range(rows):
        normed = normed_ref[r * count : (r + 1) * count, :]
        proj = lax.dot_general(
            turned, normed, (((1,), (1,)), ((), ())), preferred_element_type=F32
        )
        mask = keep_ref[r : r + 1, :]
        sides = mask * jax.nn.sigmoid(proj[2 * inner :]) * proj[: 2 * inner]
        lr_ref[:, r] = sides.reshape(peers, wide, count).astype(BF16)


def output_gates(normed_ref, w_ref, gate_ref, inner):
    step = 256
    for m in range(normed_ref.shape[0] // step):
        here = slice(m * step, (m + 1) * step)
        gate_ref[here, :] = jax.nn.sigmoid(
            jnp.dot(normed_ref[here, :], w_ref[:, 4 * inner :], preferred_element_type=F32)
        )


def prepare_kernel(
    order_ref,
    valid_ref,
    pair_ref,
    w_in_ref,
    w_back_ref,
    w_out_ref,
    z_ref,
    n_ref,
    keep_ref,
    rest_ref,
    order_s,
    valid_s,
    both_ref,
    sems,
):
    rows, count, width = z_ref.shape
    trans = w_back_ref.shape[1]
    scalars = [
        pltpu.make_async_copy(order_ref, order_s, sems.at[0]),
        pltpu.make_async_copy(valid_ref, valid_s, sems.at[1]),
    ]
    state = pltpu.make_async_copy(pair_ref, both_ref, sems.at[2])
    for copy in scalars:
        copy.start()
    state.start()
    parts = 2 * trans // width
    sources = [w_in_ref.at[0, :, pl.ds(j * width, width)] for j in range(parts)]
    sources += [w_back_ref.at[0], w_out_ref.at[0]]
    packing, at = [], 0
    for i, source in enumerate(sources):
        size = source.shape[0]
        packing.append(
            pltpu.make_async_copy(source, rest_ref.at[pl.ds(at, size)], sems.at[3 + i])
        )
        packing[-1].start()
        at += size
    for copy in scalars:
        copy.wait()
    crop = order_s[lax.axis_index("section")]
    valid = valid_s[crop]
    row = lax.axis_index("row") * rows + lax.broadcasted_iota(jnp.int32, (rows, count), 0)
    column = lax.broadcasted_iota(jnp.int32, (rows, count), 1)
    keep = jnp.logical_and(row < valid, column < valid)
    keep_ref[...] = jnp.where(keep, 1.0, 0.0)
    state.wait()
    for r in range(rows):
        here = both_ref[crop, r]
        z_ref[r] = here
        n_ref[r * count : (r + 1) * count, :] = layer_norm(here.astype(F32)).astype(BF16)
    for copy in packing:
        copy.wait()


def project_kernel(inner, n_ref, keep_ref, own_ref, other_ref, lr_ref, w_ref, sems):
    section = lax.axis_index("section")
    fetch(section == 0, own_ref.at[0], other_ref.at[0], w_ref, sems.at[0]).wait()
    project(n_ref, w_ref, keep_ref, lr_ref, inner)


def gates_kernel(inner, n_ref, own_ref, other_ref, gate_ref, w_ref, sems):
    section = lax.axis_index("section")
    fetch(section == 0, own_ref.at[0], other_ref.at[0], w_ref, sems.at[0]).wait()
    output_gates(n_ref, w_ref, gate_ref, inner)


def tri_kernel(in_ref, out_ref, wide_ref):
    peers, rows, wide, count = in_ref.shape
    share = wide // 2
    total = peers * rows
    wide_ref[...] = in_ref[...].astype(F32).reshape(total * wide, count)
    for c in range(share):
        left = wide_ref[pl.ds(c, total, stride=wide), :].astype(BF16)
        right = wide_ref[pl.ds(share + c, total, stride=wide), :].astype(BF16)
        tri = lax.dot_general(
            left, right, (((1,), (1,)), ((), ())), preferred_element_type=F32
        )
        out_ref[:, c] = tri.reshape(peers, rows, total).astype(BF16)


def update_kernel(
    block,
    blocks,
    inner,
    trans,
    keep_ref,
    tri_ref,
    gate_ref,
    z_ref,
    own_ref,
    other_ref,
    wp_own_ref,
    wp_other_ref,
    *refs,
):
    last = block == blocks - 1
    if last:
        out_ref, t_ref, w_ref, n_ref, z1_ref, sems = refs
    else:
        out_ref, lr_ref, gate_out_ref, t_ref, w_ref, n_ref, z1_ref, sems, wp_ref = refs
    section = lax.axis_index("section")
    rows, count, width = out_ref.shape
    weights = fetch(section == block, own_ref, other_ref, w_ref, sems.at[0])
    if not last:
        following = fetch(
            section == block + 1, wp_own_ref.at[0], wp_other_ref.at[0], wp_ref, sems.at[1]
        )
    parts = width * (2 * trans // width)
    t_ref[...] = layer_norm(tri_ref[...].reshape(inner, rows, count).astype(F32), 0).reshape(
        inner * rows, count
    )
    weights.wait()
    w_out = w_ref[parts + trans : parts + trans + inner, :]
    for r in range(rows):
        here = slice(r * count, (r + 1) * count)
        tri = t_ref[pl.ds(r, inner, stride=rows), :].astype(BF16)
        update = lax.dot_general(
            tri, w_out, (((0,), (0,)), ((), ())), preferred_element_type=F32
        )
        first = (z_ref[r].astype(F32) + gate_ref[here, :] * update).astype(BF16)
        z1_ref[here, :] = first
        n_ref[here, :] = layer_norm(first.astype(F32)).astype(BF16)
    step = 2 * count
    for m in range(rows * count // step):
        here = slice(m * step, (m + 1) * step)
        normed = n_ref[here, :]
        total = z1_ref[here, :].astype(F32)
        for j in range(trans // width):
            gate_w = w_ref[j * width : (j + 1) * width, :]
            up_w = w_ref[trans + j * width : trans + (j + 1) * width, :]
            gate = jnp.dot(normed, gate_w, preferred_element_type=F32)
            up = jnp.dot(normed, up_w, preferred_element_type=F32)
            act = (jax.nn.silu(gate) * up).astype(BF16)
            back_w = w_ref[parts + j * width : parts + (j + 1) * width, :]
            total = total + jnp.dot(act, back_w, preferred_element_type=F32)
        done = total.astype(BF16)
        out_ref[2 * m : 2 * m + 2] = done.reshape(2, count, width)
        if not last:
            n_ref[here, :] = layer_norm(done.astype(F32)).astype(BF16)
    if not last:
        following.wait()
        project(n_ref, wp_ref, keep_ref, lr_ref, inner)
        output_gates(n_ref, wp_ref, gate_out_ref, inner)


def fast_body(pair, valid_tokens, crop_order, w_proj, w_out, w_in, w_back):
    crops, rows, count, width = pair.shape
    peers = lax.axis_size("row")
    inner, trans = w_out.shape[1], w_back.shape[1]
    share = inner // peers
    wide = 2 * share
    blocks = lax.axis_size("section")
    swap = [(0, 1), (1, 0)]
    rest_rows = 2 * trans + trans + inner

    vmem = pl.BlockSpec(memory_space=pltpu.VMEM)
    hbm = pl.BlockSpec(memory_space=pltpu.HBM)
    anywhere = pl.BlockSpec(memory_space=pl.ANY)
    sides = jax.ShapeDtypeStruct((peers, rows, wide, count), BF16)
    gates = jax.ShapeDtypeStruct((rows * count, width), F32)
    state = jax.ShapeDtypeStruct((rows, count, width), BF16)
    tokens = jax.ShapeDtypeStruct((rows * count, width), BF16)

    wp_other = lax.ppermute(w_proj, "section", swap)
    z, normed, keep, rest = pl.pallas_call(
        prepare_kernel,
        out_shape=(
            state,
            tokens,
            jax.ShapeDtypeStruct((rows, count), F32),
            jax.ShapeDtypeStruct((rest_rows, width), BF16),
        ),
        in_specs=[hbm] * 6,
        out_specs=(vmem,) * 4,
        scratch_shapes=[
            pltpu.SMEM(crop_order.shape, jnp.int32),
            pltpu.SMEM(valid_tokens.shape, jnp.int32),
            pltpu.VMEM(pair.shape, BF16),
            pltpu.SemaphoreType.DMA((5 + 2 * trans // width,)),
        ],
        compiler_params=LIMIT,
        cost_estimate=pl.CostEstimate(flops=10**6, bytes_accessed=3 * 10**6, transcendentals=0),
        name="prepare",
    )(*[pltpu.with_memory_space_constraint(x, pltpu.HBM) for x in (crop_order, valid_tokens, pair, w_in, w_back, w_out)])
    rest_other = lax.ppermute(rest, "section", swap)

    weights = pltpu.VMEM(w_proj.shape[1:], BF16)
    lr = pl.pallas_call(
        functools.partial(project_kernel, inner),
        out_shape=sides,
        in_specs=[vmem, vmem, anywhere, anywhere],
        out_specs=vmem,
        scratch_shapes=[weights, pltpu.SemaphoreType.DMA((1,))],
        compiler_params=LIMIT,
        name="project",
    )(normed, keep, w_proj, wp_other)
    gate = pl.pallas_call(
        functools.partial(gates_kernel, inner),
        out_shape=gates,
        in_specs=[vmem, anywhere, anywhere],
        out_specs=vmem,
        scratch_shapes=[weights, pltpu.SemaphoreType.DMA((1,))],
        compiler_params=LIMIT,
        cost_estimate=pl.CostEstimate(flops=34 * 10**6, bytes_accessed=10**6, transcendentals=2 * 10**5),
        name="gates",
    )(normed, w_proj, wp_other)

    for block in range(blocks):
        last = block == blocks - 1
        whole = lax.all_to_all(lr, "row", split_axis=0, concat_axis=0, tiled=True)
        tri_part = pl.pallas_call(
            tri_kernel,
            out_shape=jax.ShapeDtypeStruct((peers, share, rows, count), BF16),
            in_specs=[vmem],
            out_specs=vmem,
            scratch_shapes=[pltpu.VMEM((peers * rows * wide, count), F32)],
            compiler_params=LIMIT,
            name="triangle",
        )(whole)
        tri = lax.all_to_all(tri_part, "row", split_axis=0, concat_axis=0, tiled=True)
        scratch = [
            pltpu.VMEM((inner * rows, count), F32),
            pltpu.VMEM((rest_rows, width), BF16),
            pltpu.VMEM((rows * count, width), BF16),
            pltpu.VMEM((rows * count, width), BF16),
            pltpu.SemaphoreType.DMA((2,)),
        ]
        if not last:
            scratch.append(pltpu.VMEM(w_proj.shape[1:], BF16))
        result = pl.pallas_call(
            functools.partial(update_kernel, block, blocks, inner, trans),
            out_shape=(state,) if last else (state, sides, gates),
            in_specs=[vmem] * 4 + [anywhere] * 4,
            out_specs=(vmem,) if last else (vmem,) * 3,
            scratch_shapes=scratch,
            compiler_params=LIMIT,
            name="update_last" if last else "update",
        )(keep, tri, gate, z, rest, rest_other, w_proj, wp_other)
        if last:
            (z,) = result
        else:
            z, lr, gate = result
    return z[None]


def pair_block(state, valid, row_start, w_proj, w_out, w_in, w_back):
    rows_here, count, width = state.shape
    inner, trans = w_out.shape[0], w_back.shape[0]
    normed = layer_norm(state.astype(F32)).astype(BF16).reshape(rows_here * count, width)
    proj = jnp.dot(normed, w_proj, preferred_element_type=F32).reshape(rows_here, count, -1)
    keep_cols = (jnp.arange(count) < valid).astype(F32)
    keep_rows = (row_start + jnp.arange(rows_here) < valid).astype(F32)
    mask = keep_rows[:, None, None] * keep_cols[None, :, None]
    left = (mask * jax.nn.sigmoid(proj[..., inner : 2 * inner]) * proj[..., :inner]).astype(BF16)
    right = (
        mask * jax.nn.sigmoid(proj[..., 3 * inner : 4 * inner]) * proj[..., 2 * inner : 3 * inner]
    ).astype(BF16)
    gate = jax.nn.sigmoid(proj[..., 4 * inner :])
    left_whole = lax.all_to_all(left, "row", split_axis=2, concat_axis=0, tiled=True)
    right_whole = lax.all_to_all(right, "row", split_axis=2, concat_axis=0, tiled=True)
    tri_part = jnp.einsum("ikc,jkc->ijc", left_whole, right_whole, preferred_element_type=F32)
    tri = lax.all_to_all(
        tri_part.astype(BF16), "row", split_axis=0, concat_axis=2, tiled=True
    ).astype(F32)
    tri_normed = layer_norm(tri).astype(BF16).reshape(rows_here * count, inner)
    update = jnp.dot(tri_normed, w_out, preferred_element_type=F32).reshape(rows_here, count, width)
    first = (state.astype(F32) + gate * update).astype(BF16)
    second = layer_norm(first.astype(F32)).astype(BF16).reshape(rows_here * count, width)
    hidden = jnp.dot(second, w_in, preferred_element_type=F32)
    act = (jax.nn.silu(hidden[:, :trans]) * hidden[:, trans:]).astype(BF16)
    back = jnp.dot(act, w_back, preferred_element_type=F32).reshape(rows_here, count, width)
    return (first.astype(F32) + back).astype(BF16)


def general_body(pair, valid_tokens, crop_order, w_proj, w_out, w_in, w_back):
    crops, rows_here = pair.shape[:2]
    row_start = lax.axis_index("row") * rows_here
    share = crops // lax.axis_size("section")
    section = lax.axis_index("section")
    weights = [
        lax.all_gather(w, "section", axis=0, tiled=True) for w in (w_proj, w_out, w_in, w_back)
    ]
    blocks = weights[0].shape[0]

    def one_crop(index, outputs):
        crop = crop_order[section * share + index]
        valid = valid_tokens[crop]
        state = lax.dynamic_index_in_dim(pair, crop, 0, keepdims=False)

        def apply_block(block, value):
            return pair_block(value, valid, row_start, *[w[block] for w in weights])

        final = lax.fori_loop(0, blocks, apply_block, state)
        return lax.dynamic_update_index_in_dim(outputs, final, index, 0)

    empty = jnp.zeros((share,) + pair.shape[1:], BF16)
    return lax.fori_loop(0, share, one_crop, empty)


def solution(mesh):
    sections, peers = mesh.shape["section"], mesh.shape["row"]

    def body(pair, valid_tokens, crop_order, w_proj, w_out, w_in, w_back):
        crops, rows, count, width = pair.shape
        inner, trans = w_out.shape[1], w_back.shape[1]
        fits = (
            sections == 2
            and crops == sections
            and w_proj.shape[0] == 1
            and rows == 8
            and count == width == 128
            and inner == 4 * peers
            and trans % width == 0
        )
        run = fast_body if fits else general_body
        return run(pair, valid_tokens, crop_order, w_proj, w_out, w_in, w_back)

    weights = P("section", None, None)
    return jax.shard_map(
        body,
        mesh=mesh,
        in_specs=(P(None, "row", None, None), P(), P(), weights, weights, weights, weights),
        out_specs=P("section", "row", None, None),
        check_vma=False,
    )
```

```python
import functools

import jax
import jax.numpy as jnp
from jax import lax
from jax.experimental import pallas as pl
from jax.experimental.pallas import tpu as pltpu
from jax.sharding import PartitionSpec as P

F32 = jnp.float32
BF16 = jnp.bfloat16
STEP = 512
LIMIT = pltpu.CompilerParams(vmem_limit_bytes=16 * 2**20)


def layer_norm(value, axis=-1):
    mean = jnp.mean(value, axis, keepdims=True)
    centred = value - mean
    var = jnp.mean(centred * centred, axis, keepdims=True)
    return centred * lax.rsqrt(var + 1e-05)


def row_norm(value):
    return layer_norm(value.astype(F32)).astype(BF16)


def ordered_weights(weights, inner, share):
    wide = 2 * share
    row = lax.broadcasted_iota(jnp.int32, (4 * inner, 4 * inner), 0)
    column = lax.broadcasted_iota(jnp.int32, (4 * inner, 4 * inner), 1)
    gates, rest = lax.div(row, 2 * inner), lax.rem(row, 2 * inner)
    peer, slot = lax.div(rest, wide), lax.rem(rest, wide)
    side, channel = lax.div(slot, share), lax.rem(slot, share)
    source = side * (2 * inner) + gates * inner + peer * share + channel
    pick = jnp.where(column == source, 1.0, 0.0).astype(BF16)
    return lax.dot_general(
        pick, weights, (((1,), (1,)), ((), ())), preferred_element_type=F32
    ).astype(BF16)


def project(normed_ref, weights, keep_ref, lr_ref, inner):
    peers, rows, wide, count = lr_ref.shape
    turned = ordered_weights(weights, inner, wide // 2)
    for r in range(rows):
        normed = normed_ref[r * count : (r + 1) * count, :]
        proj = lax.dot_general(
            turned, normed, (((1,), (1,)), ((), ())), preferred_element_type=F32
        )
        mask = keep_ref[r : r + 1, :]
        sides = mask * jax.nn.sigmoid(proj[2 * inner :]) * proj[: 2 * inner]
        lr_ref[:, r] = sides.reshape(peers, wide, count).astype(BF16)


def output_gates(normed_ref, weights, gate_ref):
    step = 256
    for m in range(normed_ref.shape[0] // step):
        here = slice(m * step, (m + 1) * step)
        gate_ref[here, :] = jax.nn.sigmoid(
            jnp.dot(normed_ref[here, :], weights, preferred_element_type=F32)
        )


def prepare_kernel(
    order_ref,
    valid_ref,
    pair_ref,
    w_in_ref,
    w_back_ref,
    w_out_ref,
    z_ref,
    n_ref,
    keep_ref,
    rest_ref,
    order_s,
    valid_s,
    both_ref,
    sems,
):
    rows, count, width = z_ref.shape
    trans = w_back_ref.shape[1]
    scalars = [
        pltpu.make_async_copy(order_ref, order_s, sems.at[0]),
        pltpu.make_async_copy(valid_ref, valid_s, sems.at[1]),
    ]
    state = pltpu.make_async_copy(pair_ref, both_ref, sems.at[2])
    for copy in scalars:
        copy.start()
    state.start()
    parts = 2 * trans // width
    sources = [w_in_ref.at[0, :, pl.ds(j * width, width)] for j in range(parts)]
    sources += [w_back_ref.at[0], w_out_ref.at[0]]
    packing, at = [], 0
    for i, source in enumerate(sources):
        size = source.shape[0]
        packing.append(
            pltpu.make_async_copy(source, rest_ref.at[pl.ds(at, size)], sems.at[3 + i])
        )
        packing[-1].start()
        at += size
    for copy in scalars:
        copy.wait()
    crop = order_s[lax.axis_index("section")]
    valid = valid_s[crop]
    row = lax.axis_index("row") * rows + lax.broadcasted_iota(jnp.int32, (rows, count), 0)
    column = lax.broadcasted_iota(jnp.int32, (rows, count), 1)
    keep = jnp.logical_and(row < valid, column < valid)
    keep_ref[...] = jnp.where(keep, 1.0, 0.0)
    state.wait()
    for r in range(rows):
        here = both_ref[crop, r]
        z_ref[r] = here
        n_ref[r * count : (r + 1) * count, :] = row_norm(here)
    for copy in packing:
        copy.wait()


def project_kernel(inner, n_ref, keep_ref, own_ref, other_ref, lr_ref):
    mine = lax.axis_index("section") == 0
    weights = jnp.where(mine, own_ref[0, :, : 4 * inner], other_ref[0, :, : 4 * inner])
    project(n_ref, weights, keep_ref, lr_ref, inner)


def gates_kernel(inner, n_ref, own_ref, other_ref, gate_ref):
    mine = lax.axis_index("section") == 0
    weights = jnp.where(mine, own_ref[0, :, 4 * inner :], other_ref[0, :, 4 * inner :])
    output_gates(n_ref, weights, gate_ref)


def tri_kernel(in_ref, out_ref, wide_ref):
    peers, rows, wide, count = in_ref.shape
    share = wide // 2
    total = peers * rows
    wide_ref[...] = in_ref[...].astype(F32).reshape(total * wide, count)
    for c in range(share):
        left = wide_ref[pl.ds(c, total, stride=wide), :].astype(BF16)
        right = wide_ref[pl.ds(share + c, total, stride=wide), :].astype(BF16)
        tri = lax.dot_general(
            left, right, (((1,), (1,)), ((), ())), preferred_element_type=F32
        )
        out_ref[:, c] = tri.reshape(peers, rows, total).astype(BF16)


def update_kernel(
    block,
    blocks,
    inner,
    trans,
    keep_ref,
    tri_ref,
    gate_ref,
    z_ref,
    own_ref,
    other_ref,
    wp_own_ref,
    wp_other_ref,
    *refs,
):
    last = block == blocks - 1
    if last:
        out_ref, t_ref, in_ref, back_ref, n_ref, z1_ref, o_ref, sems = refs
    else:
        o_ref, lr_ref, gate_out_ref, t_ref, in_ref, back_ref, n_ref, z1_ref = refs
    section = lax.axis_index("section")
    rows, count, width = o_ref.shape
    mine = section == block
    hidden, both = 2 * trans, 3 * trans

    def pick(start, size):
        here = slice(start, start + size)
        return jnp.where(mine, own_ref[here, :], other_ref[here, :])

    for j in range(hidden // width):
        in_ref[:, j * width : (j + 1) * width] = pick(j * width, width)
    back_ref[...] = pick(hidden, trans)
    w_out = pick(both, inner)
    t_ref[...] = layer_norm(tri_ref[...].reshape(inner, rows, count).astype(F32), 0).reshape(
        inner * rows, count
    )
    for r in range(rows):
        here = slice(r * count, (r + 1) * count)
        tri = t_ref[pl.ds(r, inner, stride=rows), :].astype(BF16)
        update = lax.dot_general(
            tri, w_out, (((0,), (0,)), ((), ())), preferred_element_type=F32
        )
        first = (z_ref[r].astype(F32) + gate_ref[here, :] * update).astype(BF16)
        z1_ref[here, :] = first
        n_ref[here, :] = row_norm(first)
    step, piece = STEP, 256
    copies = []
    for m in range(rows * count // step):
        here = slice(m * step, (m + 1) * step)
        normed = n_ref[here, :]
        acts = []
        for j in range(trans // piece):
            gate_w = in_ref[:, j * piece : (j + 1) * piece]
            up_w = in_ref[:, trans + j * piece : trans + (j + 1) * piece]
            gate = jnp.dot(normed, gate_w, preferred_element_type=F32)
            up = jnp.dot(normed, up_w, preferred_element_type=F32)
            acts.append((jax.nn.silu(gate) * up).astype(BF16))
        act = jnp.concatenate(acts, -1)
        back = jnp.dot(act, back_ref[...], preferred_element_type=F32)
        done = (z1_ref[here, :].astype(F32) + back).astype(BF16)
        n = step // count
        o_ref[n * m : n * (m + 1)] = done.reshape(n, count, width)
        if last:
            part = pl.ds(n * m, n)
            copies.append(pltpu.make_async_copy(o_ref.at[part], out_ref.at[part], sems.at[m]))
            copies[-1].start()
        else:
            n_ref[here, :] = row_norm(done)
    for copy in copies:
        copy.wait()
    if not last:
        following = section == block + 1
        weights = jnp.where(following, wp_own_ref[0], wp_other_ref[0])
        project(n_ref, weights[:, : 4 * inner], keep_ref, lr_ref, inner)
        output_gates(n_ref, weights[:, 4 * inner :], gate_out_ref)


def fast_body(pair, valid_tokens, crop_order, w_proj, w_out, w_in, w_back):
    crops, rows, count, width = pair.shape
    peers = lax.axis_size("row")
    inner, trans = w_out.shape[1], w_back.shape[1]
    share = inner // peers
    wide = 2 * share
    blocks = lax.axis_size("section")
    swap = [(0, 1), (1, 0)]
    rest_rows = 2 * trans + trans + inner

    vmem = pl.BlockSpec(memory_space=pltpu.VMEM)
    hbm = pl.BlockSpec(memory_space=pltpu.HBM)
    sides = jax.ShapeDtypeStruct((peers, rows, wide, count), BF16)
    gates = jax.ShapeDtypeStruct((rows * count, width), F32)
    state = jax.ShapeDtypeStruct((rows, count, width), BF16)
    tokens = jax.ShapeDtypeStruct((rows * count, width), BF16)

    wp_other = lax.ppermute(w_proj, "section", swap)
    z, normed, keep, rest = pl.pallas_call(
        prepare_kernel,
        out_shape=(
            state,
            tokens,
            jax.ShapeDtypeStruct((rows, count), F32),
            jax.ShapeDtypeStruct((rest_rows, width), BF16),
        ),
        in_specs=[hbm] * 6,
        out_specs=(vmem,) * 4,
        scratch_shapes=[
            pltpu.SMEM(crop_order.shape, jnp.int32),
            pltpu.SMEM(valid_tokens.shape, jnp.int32),
            pltpu.VMEM(pair.shape, BF16),
            pltpu.SemaphoreType.DMA((5 + 2 * trans // width,)),
        ],
        compiler_params=LIMIT,
        cost_estimate=pl.CostEstimate(flops=10**6, bytes_accessed=3 * 10**6, transcendentals=0),
        name="prepare",
    )(*[pltpu.with_memory_space_constraint(x, pltpu.HBM) for x in (crop_order, valid_tokens, pair, w_in, w_back, w_out)])
    rest_other = lax.ppermute(rest, "section", swap)

    lr = pl.pallas_call(
        functools.partial(project_kernel, inner),
        out_shape=sides,
        in_specs=[vmem] * 4,
        out_specs=vmem,
        compiler_params=LIMIT,
        name="project",
    )(normed, keep, w_proj, wp_other)
    gate = pl.pallas_call(
        functools.partial(gates_kernel, inner),
        out_shape=gates,
        in_specs=[vmem] * 3,
        out_specs=vmem,
        compiler_params=LIMIT,
        cost_estimate=pl.CostEstimate(flops=34 * 10**6, bytes_accessed=10**6, transcendentals=2 * 10**5),
        name="gates",
    )(normed, w_proj, wp_other)

    for block in range(blocks):
        last = block == blocks - 1
        whole = lax.all_to_all(lr, "row", split_axis=0, concat_axis=0, tiled=True)
        tri_part = pl.pallas_call(
            tri_kernel,
            out_shape=jax.ShapeDtypeStruct((peers, share, rows, count), BF16),
            in_specs=[vmem],
            out_specs=vmem,
            scratch_shapes=[pltpu.VMEM((peers * rows * wide, count), F32)],
            compiler_params=LIMIT,
            name="triangle",
        )(whole)
        tri = lax.all_to_all(tri_part, "row", split_axis=0, concat_axis=0, tiled=True)
        scratch = [
            pltpu.VMEM((inner * rows, count), F32),
            pltpu.VMEM(w_in.shape[1:], BF16),
            pltpu.VMEM(w_back.shape[1:], BF16),
            pltpu.VMEM(tokens.shape, BF16),
            pltpu.VMEM(tokens.shape, BF16),
        ]
        if last:
            scratch += [
                pltpu.VMEM(state.shape, BF16),
                pltpu.SemaphoreType.DMA((rows * count // STEP,)),
            ]
        result = pl.pallas_call(
            functools.partial(update_kernel, block, blocks, inner, trans),
            out_shape=(state,) if last else (state, sides, gates),
            in_specs=[vmem] * 8,
            out_specs=(hbm,) if last else (vmem,) * 3,
            scratch_shapes=scratch,
            compiler_params=LIMIT,
            name="update_last" if last else "update",
        )(keep, tri, gate, z, rest, rest_other, w_proj, wp_other)
        if last:
            (z,) = result
        else:
            z, lr, gate = result
    return z[None]


def pair_block(state, valid, row_start, w_proj, w_out, w_in, w_back):
    rows_here, count, width = state.shape
    inner, trans = w_out.shape[0], w_back.shape[0]
    normed = layer_norm(state.astype(F32)).astype(BF16).reshape(rows_here * count, width)
    proj = jnp.dot(normed, w_proj, preferred_element_type=F32).reshape(rows_here, count, -1)
    keep_cols = (jnp.arange(count) < valid).astype(F32)
    keep_rows = (row_start + jnp.arange(rows_here) < valid).astype(F32)
    mask = keep_rows[:, None, None] * keep_cols[None, :, None]
    left = (mask * jax.nn.sigmoid(proj[..., inner : 2 * inner]) * proj[..., :inner]).astype(BF16)
    right = (
        mask * jax.nn.sigmoid(proj[..., 3 * inner : 4 * inner]) * proj[..., 2 * inner : 3 * inner]
    ).astype(BF16)
    gate = jax.nn.sigmoid(proj[..., 4 * inner :])
    left_whole = lax.all_to_all(left, "row", split_axis=2, concat_axis=0, tiled=True)
    right_whole = lax.all_to_all(right, "row", split_axis=2, concat_axis=0, tiled=True)
    tri_part = jnp.einsum("ikc,jkc->ijc", left_whole, right_whole, preferred_element_type=F32)
    tri = lax.all_to_all(
        tri_part.astype(BF16), "row", split_axis=0, concat_axis=2, tiled=True
    ).astype(F32)
    tri_normed = layer_norm(tri).astype(BF16).reshape(rows_here * count, inner)
    update = jnp.dot(tri_normed, w_out, preferred_element_type=F32).reshape(rows_here, count, width)
    first = (state.astype(F32) + gate * update).astype(BF16)
    second = layer_norm(first.astype(F32)).astype(BF16).reshape(rows_here * count, width)
    hidden = jnp.dot(second, w_in, preferred_element_type=F32)
    act = (jax.nn.silu(hidden[:, :trans]) * hidden[:, trans:]).astype(BF16)
    back = jnp.dot(act, w_back, preferred_element_type=F32).reshape(rows_here, count, width)
    return (first.astype(F32) + back).astype(BF16)


def general_body(pair, valid_tokens, crop_order, w_proj, w_out, w_in, w_back):
    crops, rows_here = pair.shape[:2]
    row_start = lax.axis_index("row") * rows_here
    share = crops // lax.axis_size("section")
    section = lax.axis_index("section")
    weights = [
        lax.all_gather(w, "section", axis=0, tiled=True) for w in (w_proj, w_out, w_in, w_back)
    ]
    blocks = weights[0].shape[0]

    def one_crop(index, outputs):
        crop = crop_order[section * share + index]
        valid = valid_tokens[crop]
        state = lax.dynamic_index_in_dim(pair, crop, 0, keepdims=False)

        def apply_block(block, value):
            return pair_block(value, valid, row_start, *[w[block] for w in weights])

        final = lax.fori_loop(0, blocks, apply_block, state)
        return lax.dynamic_update_index_in_dim(outputs, final, index, 0)

    empty = jnp.zeros((share,) + pair.shape[1:], BF16)
    return lax.fori_loop(0, share, one_crop, empty)


def solution(mesh):
    sections, peers = mesh.shape["section"], mesh.shape["row"]

    def body(pair, valid_tokens, crop_order, w_proj, w_out, w_in, w_back):
        crops, rows, count, width = pair.shape
        inner, trans = w_out.shape[1], w_back.shape[1]
        fits = (
            sections == 2
            and crops == sections
            and w_proj.shape[0] == 1
            and rows == 8
            and count == width == 128
            and inner == 4 * peers
            and trans % width == 0
        )
        run = fast_body if fits else general_body
        return run(pair, valid_tokens, crop_order, w_proj, w_out, w_in, w_back)

    weights = P("section", None, None)
    return jax.shard_map(
        body,
        mesh=mesh,
        in_specs=(P(None, "row", None, None), P(), P(), weights, weights, weights, weights),
        out_specs=P("section", "row", None, None),
        check_vma=False,
    )
```

```python
import functools

import jax
import jax.numpy as jnp
from jax import lax
from jax.experimental import pallas as pl
from jax.experimental.pallas import tpu as pltpu
from jax.sharding import PartitionSpec as P

F32 = jnp.float32
BF16 = jnp.bfloat16
STEP = 512
CHANNELS = 2
SHORT = 32
LIMIT = pltpu.CompilerParams(vmem_limit_bytes=16 * 2**20)


def layer_norm(value, axis=-1):
    mean = jnp.mean(value, axis, keepdims=True)
    centred = value - mean
    var = jnp.mean(centred * centred, axis, keepdims=True)
    return centred * lax.rsqrt(var + 1e-05)


def row_norm(value):
    return layer_norm(value.astype(F32)).astype(BF16)


def contract(left, right, left_axis, right_axis):
    return lax.dot_general(
        left, right, (((left_axis,), (right_axis,)), ((), ())), preferred_element_type=F32
    )


def tile_weights(weights, inner):
    total = 8 * inner
    row = lax.broadcasted_iota(jnp.int32, (total, 4 * inner), 0)
    column = lax.broadcasted_iota(jnp.int32, (total, 4 * inner), 1)
    gates, rest = lax.div(row, 4 * inner), lax.rem(row, 4 * inner)
    peer, slot = lax.div(rest, 8), lax.rem(rest, 8)
    half, side, channel = lax.div(slot, 4), lax.rem(lax.div(slot, 2), 2), lax.rem(slot, 2)
    source = side * (2 * inner) + gates * inner + peer * CHANNELS + channel
    parts = []
    for h in range(2):
        chosen = jnp.logical_and(column == source, half == h)
        pick = jnp.where(chosen, 1.0, 0.0).astype(BF16)
        parts.append(contract(pick, weights, 1, 1).astype(BF16))
    return jnp.concatenate(parts, -1)


def put_tiles(turned, halves, masks, lr_ref, first, inner):
    peers, count = lr_ref.shape[0], lr_ref.shape[-1]
    normed = jnp.concatenate([jnp.concatenate(pair, -1) for pair in halves], 0)
    proj = contract(turned, normed, 1, 1)
    sides = jax.nn.sigmoid(proj[4 * inner :]) * proj[: 4 * inner]
    for i, mask in enumerate(masks):
        tile = sides[:, i * count : (i + 1) * count].reshape(peers, 8, count)
        lr_ref[:, first + i] = (tile * mask[None]).astype(BF16)


def full_mask(row, valid, count):
    half = lax.div(lax.broadcasted_iota(jnp.int32, (8, count), 0), 4)
    token = lax.broadcasted_iota(jnp.int32, (8, count), 1)
    return jnp.where(jnp.logical_and(row + half < valid, token < valid), 1.0, 0.0)


def short_mask(row, valid, count):
    half = lax.div(lax.broadcasted_iota(jnp.int32, (8, count), 0), 4)
    lane = lax.broadcasted_iota(jnp.int32, (8, count), 1)
    inside = row + 4 * half + lax.div(lane, SHORT) < valid
    return jnp.where(jnp.logical_and(inside, lax.rem(lane, SHORT) < valid), 1.0, 0.0)


def read_scalars(order_ref, valid_ref, order_s, valid_s, sems):
    copies = [
        pltpu.make_async_copy(order_ref, order_s, sems.at[0]),
        pltpu.make_async_copy(valid_ref, valid_s, sems.at[1]),
    ]
    for copy in copies:
        copy.start()
    return copies


def first_kernel(
    inner,
    order_ref,
    valid_ref,
    pair_ref,
    wp_ref,
    w_in_ref,
    w_back_ref,
    w_out_ref,
    lr_ref,
    pack_ref,
    z_ref,
    owns_ref,
    masks_ref,
    order_s,
    valid_s,
    both_ref,
    w_ref,
    sems,
):
    rows, count, width = pair_ref.shape[1:]
    trans = w_back_ref.shape[1]
    scalars = read_scalars(order_ref, valid_ref, order_s, valid_s, sems)
    weights = pltpu.make_async_copy(wp_ref.at[0], w_ref, sems.at[2])
    weights.start()
    state = pltpu.make_async_copy(pair_ref, both_ref, sems.at[3])
    state.start()
    sources = [w_in_ref.at[0, :, pl.ds(j * width, width)] for j in range(2 * trans // width)]
    sources += [w_back_ref.at[0], w_out_ref.at[0]]
    sources += [wp_ref.at[0, :, pl.ds(j * width, width)] for j in range(w_ref.shape[1] // width)]
    packing, at = [], 0
    for i, source in enumerate(sources):
        size = source.shape[0]
        packing.append(
            pltpu.make_async_copy(source, pack_ref.at[pl.ds(at, size)], sems.at[4 + i])
        )
        packing[-1].start()
        at += size
    weights.wait()
    turned = tile_weights(w_ref[:, : 4 * inner], inner)
    for copy in scalars:
        copy.wait()
    section = lax.axis_index("section")
    full = jnp.where(valid_s[1] > valid_s[0], 1, 0)
    short = 1 - full
    owns_ref[...] = jnp.full(owns_ref.shape, jnp.where(order_s[section] == full, 1.0, 0.0))
    start = lax.axis_index("row") * rows
    mine = start + (rows // 2) * section
    masks_ref[0] = full_mask(mine, valid_s[full], count)
    masks_ref[1] = full_mask(mine + 2, valid_s[full], count)
    masks_ref[2] = short_mask(mine, valid_s[short], count)
    state.wait()
    half = pl.ds((rows // 2) * section, rows // 2)
    z_ref[: rows // 2] = both_ref[full, half]
    z_ref[rows // 2 :] = both_ref[short, half]
    for t in range(0, rows // 2, 2):
        normed = [row_norm(both_ref[full, 2 * t + r]) for r in range(4)]
        put_tiles(
            turned,
            [normed[:2], normed[2:]],
            [full_mask(start + 2 * t + r, valid_s[full], count) for r in (0, 2)],
            lr_ref,
            t,
            inner,
        )
    fours = [
        row_norm(both_ref[short, 4 * h : 4 * h + 4, :SHORT].reshape(4 * SHORT, width))
        for h in range(2)
    ]
    put_tiles(turned, [fours], [short_mask(start, valid_s[short], count)], lr_ref, rows // 2, inner)
    for copy in packing:
        copy.wait()


def short_triangle(left, right, place_ref):
    count = left.shape[1]
    block = lax.div(lax.broadcasted_iota(jnp.int32, left.shape, 1), SHORT)
    lefts = jnp.concatenate([jnp.where(block == q, left, 0.0) for q in range(4)], 0)
    rights = jnp.concatenate(
        [right if q == 0 else pltpu.roll(right, SHORT * q, 1) for q in range(4)], 0
    )
    product = contract(lefts.astype(BF16), rights.astype(BF16), 1, 1).astype(BF16)
    source = lax.broadcasted_iota(jnp.int32, (32, count), 0)
    target = lax.broadcasted_iota(jnp.int32, (32, count), 1)
    moved, token = lax.div(source, 8), lax.rem(source, 8)
    for q in range(4):
        lane = 4 * token + lax.rem(q - moved + 4, 4)
        pick = jnp.where(target == lane, 1.0, 0.0).astype(BF16)
        place_ref[pl.ds(q, 8, stride=4), :] = jnp.dot(
            product[8 * q : 8 * q + 8], pick, preferred_element_type=F32
        )


def triangles(wide_ref, few_ref, few_stride, place_ref, count):
    results = []
    for c in range(CHANNELS):
        left = wide_ref[pl.ds(c, count, stride=4), :].astype(BF16)
        right = wide_ref[pl.ds(2 + c, count, stride=4), :].astype(BF16)
        short_triangle(
            few_ref[pl.ds(c, 8, stride=few_stride), :],
            few_ref[pl.ds(2 + c, 8, stride=few_stride), :],
            place_ref.at[c],
        )
        results.append((contract(left, right, 1, 1), place_ref[c]))
    return results


def first_triangle_kernel(in_ref, out_ref, wide_ref, few_ref, place_ref):
    peers, count = in_ref.shape[0], in_ref.shape[-1]
    rows = peers // 2
    tiles = in_ref.shape[1] - 1
    wide_ref[...] = in_ref[:rows, :tiles].astype(F32).reshape(rows * tiles * 8, count)
    few_ref[...] = in_ref[:4, tiles].astype(F32).reshape(32, count)
    results = triangles(wide_ref, few_ref, 4, place_ref, count)
    for q in range(2):
        one, two = [r[q].reshape(-1, 8, count) for r in results]
        low = lax.broadcasted_iota(jnp.int32, one.shape, 1) < 4
        groups = one.shape[0]
        tiles = (
            jnp.where(low, one, pltpu.roll(two, 4, 1)),
            jnp.where(low, pltpu.roll(one, 4, 1), two),
        )
        for section, tile in enumerate(tiles):
            out_ref[section * rows : section * rows + groups, q] = tile.astype(BF16)
            if groups < rows:
                out_ref[section * rows + groups : (section + 1) * rows, q] = jnp.zeros(
                    (rows - groups, 8, count), BF16
                )


def last_triangle_kernel(in_ref, owns_ref, out_ref, wide_ref, few_ref, place_ref):
    peers, count = in_ref.shape[0], in_ref.shape[-1]
    rows = peers // 2
    for r in range(rows):
        for section in range(2):
            at = 2 * r + section
            tiles = in_ref[section * rows + r]
            wide_ref[16 * at : 16 * at + 16, :] = tiles[:2].astype(F32).reshape(16, count)
            if at < 8:
                few_ref[8 * at : 8 * at + 8, :] = tiles[2].astype(F32)
    zero_owns = jnp.where(lax.axis_index("section") == 0, owns_ref[...], 1.0 - owns_ref[...]) > 0.5
    results = triangles(wide_ref, few_ref, 8, place_ref, count)
    for c, (full, short) in enumerate(results):
        full = full.reshape(rows, 8, count)
        short = short.reshape(-1, 8, count)
        groups = short.shape[0]
        for section in range(2):
            is_full = zero_owns if section == 0 else jnp.logical_not(zero_owns)
            at = section * rows
            out_ref[at : at + groups, c] = jnp.where(is_full[None], full[:groups], short).astype(BF16)
            out_ref[at + groups : at + rows, c] = jnp.where(
                is_full[None], full[groups:], 0.0
            ).astype(BF16)


def picker(block, own_ref, other_ref):
    mine = lax.axis_index("section") == block

    def pick(start, size):
        here = slice(start, start + size)
        return jnp.where(mine, own_ref[here, :], other_ref[here, :])

    return pick


def gates_kernel(block, inner, trans, z_ref, own_ref, other_ref, gate_ref):
    rows, count, width = z_ref.shape
    pick = picker(block, own_ref, other_ref)
    weights = pick(3 * trans + inner + 2 * width, width)
    for r in range(0, rows, 2):
        normed = row_norm(z_ref[r : r + 2].reshape(2 * count, width))
        gate_ref[r * count : (r + 2) * count, :] = jax.nn.sigmoid(
            jnp.dot(normed, weights, preferred_element_type=F32)
        )


def join_kernel(keep_ref, other_ref, z_ref):
    half = keep_ref.shape[0]
    first = lax.axis_index("section") == 0
    z_ref[:half] = jnp.where(first, keep_ref[...], other_ref[...])
    z_ref[half:] = jnp.where(first, other_ref[...], keep_ref[...])


def out_project(t_ref, offsets, stride, z_ref, gate_ref, w_out, z1_ref, n_ref):
    rows, count, width = z_ref.shape
    inner = w_out.shape[0]
    for r in range(rows):
        here = slice(r * count, (r + 1) * count)
        tri = t_ref[pl.ds(offsets[r], inner, stride=stride), :].astype(BF16)
        update = contract(tri, w_out, 0, 0)
        first = (z_ref[r].astype(F32) + gate_ref[here, :] * update).astype(BF16)
        z1_ref[here, :] = first
        n_ref[here, :] = row_norm(first)


def transition(pick, trans, in_ref, back_ref, n_ref, z1_ref, width, finish):
    hidden = 2 * trans
    for j in range(hidden // width):
        in_ref[:, j * width : (j + 1) * width] = pick(j * width, width)
    back_ref[...] = pick(hidden, trans)

    def run():
        piece = 256
        for m in range(n_ref.shape[0] // STEP):
            here = slice(m * STEP, (m + 1) * STEP)
            normed = n_ref[here, :]
            acts = []
            for j in range(trans // piece):
                gate_w = in_ref[:, j * piece : (j + 1) * piece]
                up_w = in_ref[:, trans + j * piece : trans + (j + 1) * piece]
                gate = jnp.dot(normed, gate_w, preferred_element_type=F32)
                up = jnp.dot(normed, up_w, preferred_element_type=F32)
                acts.append((jax.nn.silu(gate) * up).astype(BF16))
            back = jnp.dot(jnp.concatenate(acts, -1), back_ref[...], preferred_element_type=F32)
            finish(m, (z1_ref[here, :].astype(F32) + back).astype(BF16))

    return run


def update_kernel(
    inner,
    trans,
    tri_ref,
    gate_ref,
    z_ref,
    own_ref,
    other_ref,
    masks_ref,
    owns_ref,
    lr_ref,
    keep_ref,
    send_ref,
    t_ref,
    in_ref,
    back_ref,
    n_ref,
    z1_ref,
    o_ref,
):
    rows, count, width = z_ref.shape
    half = rows // 2
    pick = picker(0, own_ref, other_ref)

    def finish(m, done):
        o_ref[m * STEP : (m + 1) * STEP, :] = done

    run = transition(pick, trans, in_ref, back_ref, n_ref, z1_ref, width, finish)
    for q in range(2):
        part = tri_ref[:, q].astype(F32)

        def mean(value):
            total = jnp.sum(value, 0)
            return (total + pltpu.roll(total, 4, 0)) * (1.0 / inner)

        centred = part - mean(part)[None]
        var = mean(centred * centred)
        normed = centred * lax.rsqrt(var + 1e-05)[None]
        t_ref[q * 4 * inner : (q + 1) * 4 * inner, :] = normed.reshape(4 * inner, count)
    offsets = [q * 4 * inner + r for q in range(2) for r in range(half)]
    out_project(t_ref, offsets, 4, z_ref, gate_ref, pick(3 * trans, inner), z1_ref, n_ref)
    run()
    owns = (owns_ref[:1, :] > 0.5)[None]
    full = o_ref[: half * count, :].reshape(half, count, width)
    short = o_ref[half * count :, :].reshape(half, count, width)
    keep_ref[...] = jnp.where(owns, full.astype(F32), short.astype(F32)).astype(BF16)
    send_ref[...] = jnp.where(owns, short.astype(F32), full.astype(F32)).astype(BF16)
    next_pick = picker(1, own_ref, other_ref)
    at = 3 * trans + inner
    weights = jnp.concatenate([next_pick(at, width), next_pick(at + width, width)], -1)
    turned = tile_weights(weights, inner)
    normed = [row_norm(o_ref[r * count : (r + 1) * count, :]) for r in range(half)]
    put_tiles(
        turned, [normed[:2], normed[2:]], [masks_ref[0], masks_ref[1]], lr_ref, 0, inner
    )
    four = row_norm(
        jnp.concatenate(
            [o_ref[r * count : r * count + SHORT, :] for r in range(half, rows)], 0
        )
    )
    put_tiles(turned, [[four, jnp.zeros_like(four)]], [masks_ref[2]], lr_ref, 2, inner)


def last_kernel(
    inner,
    trans,
    tri_ref,
    gate_ref,
    z_ref,
    own_ref,
    other_ref,
    out_ref,
    t_ref,
    in_ref,
    back_ref,
    n_ref,
    z1_ref,
    o_ref,
    sems,
):
    rows, count, width = z_ref.shape
    pick = picker(1, own_ref, other_ref)
    copies = []

    def finish(m, done):
        part = pl.ds(m * (STEP // count), STEP // count)
        o_ref[m * (STEP // count) : (m + 1) * (STEP // count)] = done.reshape(-1, count, width)
        copies.append(pltpu.make_async_copy(o_ref.at[part], out_ref.at[part], sems.at[m]))
        copies[-1].start()

    run = transition(pick, trans, in_ref, back_ref, n_ref, z1_ref, width, finish)
    t_ref[...] = layer_norm(tri_ref[...].reshape(inner, rows, count).astype(F32), 0).reshape(
        inner * rows, count
    )
    out_project(
        t_ref, range(rows), rows, z_ref, gate_ref, pick(3 * trans, inner), z1_ref, n_ref
    )
    run()
    for copy in copies:
        copy.wait()


def fast_body(pair, valid_tokens, crop_order, w_proj, w_out, w_in, w_back):
    crops, rows, count, width = pair.shape
    devices = lax.axis_size("section") * lax.axis_size("row")
    inner, trans = w_out.shape[1], w_back.shape[1]
    swap = [(0, 1), (1, 0)]
    packed = 3 * trans + inner + w_proj.shape[2]

    vmem = pl.BlockSpec(memory_space=pltpu.VMEM)
    hbm = pl.BlockSpec(memory_space=pltpu.HBM)
    shape = jax.ShapeDtypeStruct
    flat = pltpu.VMEM((rows * count, width), BF16)
    gates = shape((rows * count, width), F32)
    sems = pltpu.SemaphoreType.DMA

    def call(kernel, name, out_shape, n_in, scratch=(), out_specs=None, in_spec=vmem, cost=None):
        many = isinstance(out_shape, tuple)
        specs = out_specs or ((vmem,) * len(out_shape) if many else vmem)
        return pl.pallas_call(
            kernel,
            out_shape=out_shape,
            in_specs=[in_spec] * n_in,
            out_specs=specs,
            scratch_shapes=list(scratch),
            compiler_params=LIMIT,
            cost_estimate=cost,
            name=name,
        )

    def exchange(value):
        return lax.all_to_all(value, ("section", "row"), split_axis=0, concat_axis=0, tiled=True)

    inputs = (crop_order, valid_tokens, pair, w_proj, w_in, w_back, w_out)
    lr, own, z, owns, masks = call(
        functools.partial(first_kernel, inner),
        "first",
        (
            shape((devices, rows // 2 + 1, 8, count), BF16),
            shape((packed, width), BF16),
            shape((rows, count, width), BF16),
            shape((8, count), F32),
            shape((3, 8, count), F32),
        ),
        len(inputs),
        [
            pltpu.SMEM(crop_order.shape, jnp.int32),
            pltpu.SMEM(valid_tokens.shape, jnp.int32),
            pltpu.VMEM(pair.shape, BF16),
            pltpu.VMEM(w_proj.shape[1:], BF16),
            sems((6 + (2 * trans + w_proj.shape[2]) // width,)),
        ],
        in_spec=hbm,
    )(*[pltpu.with_memory_space_constraint(x, pltpu.HBM) for x in inputs])

    sides = exchange(lr)
    other = lax.ppermute(own, "section", swap)
    light = pl.CostEstimate(flops=34 * 10**6, bytes_accessed=10**6, transcendentals=2 * 10**5)
    gate = call(
        functools.partial(gates_kernel, 0, inner, trans), "gates", gates, 3, cost=light
    )(z, own, other)
    tri_scratch = [
        pltpu.VMEM((4 * count, count), F32),
        pltpu.VMEM((32, count), F32),
        pltpu.VMEM((CHANNELS, 32, count), F32),
    ]
    tri = exchange(
        call(
            first_triangle_kernel, "triangle", shape((devices, 2, 8, count), BF16), 1, tri_scratch
        )(sides)
    )
    work = [
        pltpu.VMEM((8 * inner, count), F32),
        pltpu.VMEM(w_in.shape[1:], BF16),
        pltpu.VMEM(w_back.shape[1:], BF16),
        flat,
        flat,
    ]
    halves = shape((rows // 2, count, width), BF16)
    lr, keep, send = call(
        functools.partial(update_kernel, inner, trans),
        "update",
        (shape((devices, 3, 8, count), BF16), halves, halves),
        7,
        work + [flat],
    )(tri, gate, z, own, other, masks, owns)

    sides = exchange(lr)
    came = lax.ppermute(send, "section", swap)
    z = call(join_kernel, "join", shape((rows, count, width), BF16), 2)(keep, came)
    gate = call(
        functools.partial(gates_kernel, 1, inner, trans), "gates_last", gates, 3, cost=light
    )(z, own, other)
    tri_scratch[1] = pltpu.VMEM((64, count), F32)
    tri = exchange(
        call(
            last_triangle_kernel,
            "triangle_last",
            shape((devices, CHANNELS, 8, count), BF16),
            2,
            tri_scratch,
        )(sides, owns)
    )
    out = call(
        functools.partial(last_kernel, inner, trans),
        "last",
        shape((rows, count, width), BF16),
        5,
        work + [pltpu.VMEM((rows, count, width), BF16), sems((rows * count // STEP,))],
        out_specs=hbm,
    )(tri, gate, z, own, other)
    return out[None]


def pair_block(state, valid, row_start, w_proj, w_out, w_in, w_back):
    rows_here, count, width = state.shape
    inner, trans = w_out.shape[0], w_back.shape[0]
    normed = layer_norm(state.astype(F32)).astype(BF16).reshape(rows_here * count, width)
    proj = jnp.dot(normed, w_proj, preferred_element_type=F32).reshape(rows_here, count, -1)
    keep_cols = (jnp.arange(count) < valid).astype(F32)
    keep_rows = (row_start + jnp.arange(rows_here) < valid).astype(F32)
    mask = keep_rows[:, None, None] * keep_cols[None, :, None]
    left = (mask * jax.nn.sigmoid(proj[..., inner : 2 * inner]) * proj[..., :inner]).astype(BF16)
    right = (
        mask * jax.nn.sigmoid(proj[..., 3 * inner : 4 * inner]) * proj[..., 2 * inner : 3 * inner]
    ).astype(BF16)
    gate = jax.nn.sigmoid(proj[..., 4 * inner :])
    left_whole = lax.all_to_all(left, "row", split_axis=2, concat_axis=0, tiled=True)
    right_whole = lax.all_to_all(right, "row", split_axis=2, concat_axis=0, tiled=True)
    tri_part = jnp.einsum("ikc,jkc->ijc", left_whole, right_whole, preferred_element_type=F32)
    tri = lax.all_to_all(
        tri_part.astype(BF16), "row", split_axis=0, concat_axis=2, tiled=True
    ).astype(F32)
    tri_normed = layer_norm(tri).astype(BF16).reshape(rows_here * count, inner)
    update = jnp.dot(tri_normed, w_out, preferred_element_type=F32).reshape(rows_here, count, width)
    first = (state.astype(F32) + gate * update).astype(BF16)
    second = layer_norm(first.astype(F32)).astype(BF16).reshape(rows_here * count, width)
    hidden = jnp.dot(second, w_in, preferred_element_type=F32)
    act = (jax.nn.silu(hidden[:, :trans]) * hidden[:, trans:]).astype(BF16)
    back = jnp.dot(act, w_back, preferred_element_type=F32).reshape(rows_here, count, width)
    return (first.astype(F32) + back).astype(BF16)


def general_body(pair, valid_tokens, crop_order, w_proj, w_out, w_in, w_back):
    crops, rows_here = pair.shape[:2]
    row_start = lax.axis_index("row") * rows_here
    share = crops // lax.axis_size("section")
    section = lax.axis_index("section")
    weights = [
        lax.all_gather(w, "section", axis=0, tiled=True) for w in (w_proj, w_out, w_in, w_back)
    ]
    blocks = weights[0].shape[0]

    def one_crop(index, outputs):
        crop = crop_order[section * share + index]
        valid = valid_tokens[crop]
        state = lax.dynamic_index_in_dim(pair, crop, 0, keepdims=False)

        def apply_block(block, value):
            return pair_block(value, valid, row_start, *[w[block] for w in weights])

        final = lax.fori_loop(0, blocks, apply_block, state)
        return lax.dynamic_update_index_in_dim(outputs, final, index, 0)

    empty = jnp.zeros((share,) + pair.shape[1:], BF16)
    return lax.fori_loop(0, share, one_crop, empty)


def solution(mesh):
    sections, peers = mesh.shape["section"], mesh.shape["row"]

    def body(pair, valid_tokens, crop_order, w_proj, w_out, w_in, w_back):
        crops, rows, count, width = pair.shape
        inner, trans = w_out.shape[1], w_back.shape[1]
        fits = (
            sections == 2
            and crops == sections
            and w_proj.shape[0] == 1
            and rows == 8
            and count == width == 4 * SHORT
            and peers * rows == count
            and inner == 2 * CHANNELS * peers
            and w_proj.shape[2] == 3 * width
            and trans % 256 == 0
        )
        run = fast_body if fits else general_body
        return run(pair, valid_tokens, crop_order, w_proj, w_out, w_in, w_back)

    weights = P("section", None, None)
    return jax.shard_map(
        body,
        mesh=mesh,
        in_specs=(P(None, "row", None, None), P(), P(), weights, weights, weights, weights),
        out_specs=P("section", "row", None, None),
        check_vma=False,
    )
```

```python
import functools

import jax
import jax.numpy as jnp
from jax import lax
from jax.experimental import pallas as pl
from jax.experimental.pallas import tpu as pltpu
from jax.sharding import PartitionSpec as P


F32 = jnp.float32
BF16 = jnp.bfloat16
STEP = 512
CHANNELS = 2
SHORT = 32
LIMIT = pltpu.CompilerParams(vmem_limit_bytes=16 * 2**20)


def layer_norm(value, axis=-1):
    mean = jnp.mean(value, axis, keepdims=True)
    centred = value - mean
    var = jnp.mean(centred * centred, axis, keepdims=True)
    return centred * lax.rsqrt(var + 1e-05)


def row_norm(value):
    return layer_norm(value.astype(F32)).astype(BF16)


def contract(left, right, left_axis, right_axis):
    return lax.dot_general(
        left, right, (((left_axis,), (right_axis,)), ((), ())), preferred_element_type=F32
    )


def tile_weights(weights, inner):
    row = lax.broadcasted_iota(jnp.int32, (4 * inner, 2 * inner), 0)
    column = lax.broadcasted_iota(jnp.int32, (4 * inner, 2 * inner), 1)
    peer, slot = lax.div(row, 8), lax.rem(row, 4)
    source = lax.div(slot, 2) * inner + peer * CHANNELS + lax.rem(slot, 2)
    pick = jnp.where(column == source, 1.0, 0.0).astype(BF16)
    left, right = weights[:, : 2 * inner].astype(F32), weights[:, 2 * inner :].astype(F32)
    low = lax.broadcasted_iota(jnp.int32, left.shape, 1) < inner
    values = jnp.where(low, left, pltpu.roll(right, inner, 1)).astype(BF16)
    gates = jnp.where(low, pltpu.roll(left, inner, 1), right).astype(BF16)
    both = [contract(pick, part, 1, 1) for part in (values, gates)]
    half = lax.rem(lax.broadcasted_iota(jnp.int32, both[0].shape, 0), 8) < 4
    return jnp.concatenate(
        [
            jnp.concatenate([jnp.where(half, part, 0.0), jnp.where(half, 0.0, part)], -1)
            for part in both
        ],
        0,
    ).astype(BF16)


def put_tiles(turned, halves, masks, lr_ref, first, inner):
    peers, count = lr_ref.shape[0], lr_ref.shape[-1]
    normed = jnp.concatenate([jnp.concatenate(pair, -1) for pair in halves], 0)
    proj = contract(turned, normed, 1, 1)
    sides = jax.nn.sigmoid(proj[4 * inner :]) * proj[: 4 * inner]
    for i, mask in enumerate(masks):
        tile = sides[:, i * count : (i + 1) * count].reshape(peers, 8, count)
        lr_ref[:, first + i] = (tile * mask[None]).astype(BF16)


def full_mask(row, valid, count):
    half = lax.div(lax.broadcasted_iota(jnp.int32, (8, count), 0), 4)
    token = lax.broadcasted_iota(jnp.int32, (8, count), 1)
    return jnp.where(jnp.logical_and(row + half < valid, token < valid), 1.0, 0.0)


def short_mask(row, valid, count):
    half = lax.div(lax.broadcasted_iota(jnp.int32, (8, count), 0), 4)
    lane = lax.broadcasted_iota(jnp.int32, (8, count), 1)
    inside = row + 4 * half + lax.div(lane, SHORT) < valid
    return jnp.where(jnp.logical_and(inside, lax.rem(lane, SHORT) < valid), 1.0, 0.0)


def read_scalars(order_ref, valid_ref, order_s, valid_s, sems):
    copies = [
        pltpu.make_async_copy(order_ref, order_s, sems.at[0]),
        pltpu.make_async_copy(valid_ref, valid_s, sems.at[1]),
    ]
    for copy in copies:
        copy.start()
    return copies


def first_kernel(
    inner, order_ref, valid_ref, pair_ref, wp_ref, out_ref, lr_ref, order_s, valid_s, both_ref, w_ref, sems
):
    rows, count, width = pair_ref.shape[1:]
    copies = []

    def send(first, tiles):
        part = pl.ds(first, tiles)
        copies.append(
            pltpu.make_async_copy(lr_ref.at[:, part], out_ref.at[:, part], sems.at[4 + len(copies)])
        )
        copies[-1].start()

    @pl.when(lax.axis_index("section") == 0)
    def _():
        weights = pltpu.make_async_copy(wp_ref.at[0], w_ref, sems.at[2])
        weights.start()
        state = pltpu.make_async_copy(pair_ref, both_ref, sems.at[3])
        state.start()
        scalars = read_scalars(order_ref, valid_ref, order_s, valid_s, sems)
        weights.wait()
        turned = tile_weights(w_ref[:, : 4 * inner], inner)
        for copy in scalars:
            copy.wait()
        full = jnp.where(valid_s[1] > valid_s[0], 1, 0)
        short = 1 - full
        start = lax.axis_index("row") * rows
        state.wait()
        for t in range(0, rows // 2, 2):
            normed = [row_norm(both_ref[full, 2 * t + r]) for r in range(4)]
            put_tiles(
                turned,
                [normed[:2], normed[2:]],
                [full_mask(start + 2 * t + r, valid_s[full], count) for r in (0, 2)],
                lr_ref,
                t,
                inner,
            )
            send(t, 2)
        fours = [
            row_norm(both_ref[short, 4 * h : 4 * h + 4, :SHORT].reshape(4 * SHORT, width))
            for h in range(2)
        ]
        put_tiles(
            turned, [fours], [short_mask(start, valid_s[short], count)], lr_ref, rows // 2, inner
        )
        send(rows // 2, 1)
        for copy in copies:
            copy.wait()


def stage_kernel(
    order_ref,
    valid_ref,
    pair_ref,
    wp_ref,
    w_in_ref,
    w_back_ref,
    w_out_ref,
    after_ref,
    pack_ref,
    z_ref,
    n_ref,
    owns_ref,
    masks_ref,
    order_s,
    valid_s,
    both_ref,
    sems,
):
    rows, count, width = z_ref.shape
    trans = w_back_ref.shape[1]
    sources = [w_in_ref.at[0, :, pl.ds(j * width, width)] for j in range(2 * trans // width)]
    sources += [w_back_ref.at[0], w_out_ref.at[0]]
    sources += [wp_ref.at[0, :, pl.ds(j * width, width)] for j in range(wp_ref.shape[2] // width)]
    packing, at = [], 0
    for i, source in enumerate(sources):
        size = source.shape[0]
        packing.append(
            pltpu.make_async_copy(source, pack_ref.at[pl.ds(at, size)], sems.at[3 + i])
        )
        packing[-1].start()
        at += size
    scalars = read_scalars(order_ref, valid_ref, order_s, valid_s, sems)
    state = pltpu.make_async_copy(pair_ref, both_ref, sems.at[2])
    state.start()
    for copy in scalars:
        copy.wait()
    section = lax.axis_index("section")
    full = jnp.where(valid_s[1] > valid_s[0], 1, 0)
    short = 1 - full
    owns_ref[...] = jnp.full(owns_ref.shape, jnp.where(order_s[section] == full, 1.0, 0.0))
    mine = lax.axis_index("row") * rows + (rows // 2) * section
    masks_ref[0] = full_mask(mine, valid_s[full], count)
    masks_ref[1] = full_mask(mine + 2, valid_s[full], count)
    masks_ref[2] = short_mask(mine, valid_s[short], count)
    state.wait()
    half = pl.ds((rows // 2) * section, rows // 2)
    z_ref[: rows // 2] = both_ref[full, half]
    z_ref[rows // 2 :] = both_ref[short, half]
    rows_norm(z_ref, n_ref)
    for copy in packing:
        copy.wait()


def short_triangle(left, right, place_ref):
    count = left.shape[1]
    block = lax.div(lax.broadcasted_iota(jnp.int32, left.shape, 1), SHORT)
    lefts = jnp.concatenate([jnp.where(block == q, left, 0.0) for q in range(4)], 0)
    rights = jnp.concatenate(
        [right if q == 0 else pltpu.roll(right, SHORT * q, 1) for q in range(4)], 0
    )
    product = contract(lefts.astype(BF16), rights.astype(BF16), 1, 1).astype(BF16)
    source = lax.broadcasted_iota(jnp.int32, (32, count), 0)
    target = lax.broadcasted_iota(jnp.int32, (32, count), 1)
    moved, token = lax.div(source, 8), lax.rem(source, 8)
    for q in range(4):
        lane = 4 * token + lax.rem(q - moved + 4, 4)
        pick = jnp.where(target == lane, 1.0, 0.0).astype(BF16)
        place_ref[pl.ds(q, 8, stride=4), :] = jnp.dot(
            product[8 * q : 8 * q + 8], pick, preferred_element_type=F32
        )


def triangles(wide_ref, few_ref, few_stride, place_ref, count):
    results = []
    for c in range(CHANNELS):
        left = wide_ref[pl.ds(c, count, stride=4), :].astype(BF16)
        right = wide_ref[pl.ds(2 + c, count, stride=4), :].astype(BF16)
        short_triangle(
            few_ref[pl.ds(c, 8, stride=few_stride), :],
            few_ref[pl.ds(2 + c, 8, stride=few_stride), :],
            place_ref.at[c],
        )
        results.append((contract(left, right, 1, 1), place_ref[c]))
    return results


def first_triangle_kernel(in_ref, after_ref, out_ref, wide_ref, few_ref, place_ref):
    peers, count = in_ref.shape[0], in_ref.shape[-1]
    rows = peers // 2
    tiles = in_ref.shape[1] - 1
    wide_ref[...] = in_ref[:rows, :tiles].astype(F32).reshape(rows * tiles * 8, count)
    few_ref[...] = in_ref[:4, tiles].astype(F32).reshape(32, count)
    results = triangles(wide_ref, few_ref, 4, place_ref, count)
    for q in range(2):
        one, two = [r[q].reshape(-1, 8, count) for r in results]
        low = lax.broadcasted_iota(jnp.int32, one.shape, 1) < 4
        groups = one.shape[0]
        tiles = (
            jnp.where(low, one, pltpu.roll(two, 4, 1)),
            jnp.where(low, pltpu.roll(one, 4, 1), two),
        )
        for section, tile in enumerate(tiles):
            out_ref[section * rows : section * rows + groups, q] = tile.astype(BF16)
            if groups < rows:
                out_ref[section * rows + groups : (section + 1) * rows, q] = jnp.zeros(
                    (rows - groups, 8, count), BF16
                )


def last_triangle_kernel(in_ref, owns_ref, out_ref, wide_ref, few_ref, place_ref):
    peers, count = in_ref.shape[0], in_ref.shape[-1]
    rows = peers // 2
    for r in range(rows):
        for section in range(2):
            at = 2 * r + section
            tiles = in_ref[section * rows + r]
            wide_ref[16 * at : 16 * at + 16, :] = tiles[:2].astype(F32).reshape(16, count)
            if at < 8:
                few_ref[8 * at : 8 * at + 8, :] = tiles[2].astype(F32)
    zero_owns = jnp.where(lax.axis_index("section") == 0, owns_ref[...], 1.0 - owns_ref[...]) > 0.5
    results = triangles(wide_ref, few_ref, 8, place_ref, count)
    for c, (full, short) in enumerate(results):
        full = full.reshape(rows, 8, count)
        short = short.reshape(-1, 8, count)
        groups = short.shape[0]
        for section in range(2):
            is_full = zero_owns if section == 0 else jnp.logical_not(zero_owns)
            at = section * rows
            out_ref[at : at + groups, c] = jnp.where(is_full[None], full[:groups], short).astype(BF16)
            out_ref[at + groups : at + rows, c] = jnp.where(
                is_full[None], full[groups:], 0.0
            ).astype(BF16)


def picker(block, own_ref, other_ref):
    mine = lax.axis_index("section") == block

    def pick(start, size):
        here = slice(start, start + size)
        return jnp.where(mine, own_ref[here, :], other_ref[here, :])

    return pick


def ready_kernel(block, inner, trans, n_ref, own_ref, other_ref, after_ref, gate_ref, in_ref, back_ref, w_out_ref, *more):
    count = width = n_ref.shape[1]
    rows = n_ref.shape[0] // count
    pick = picker(block, own_ref, other_ref)
    projections = 3 * trans + inner
    weights = pick(projections + 2 * width, width)
    for r in range(0, rows, 4):
        here = slice(r * count, (r + 4) * count)
        gate_ref[here, :] = jax.nn.sigmoid(
            jnp.dot(n_ref[here, :], weights, preferred_element_type=F32)
        )
    for j in range(2 * trans // width):
        in_ref[:, j * width : (j + 1) * width] = pick(j * width, width)
    back_ref[...] = pick(2 * trans, trans)
    w_out_ref[...] = pick(3 * trans, inner)
    if more:
        pick = picker(block + 1, own_ref, other_ref)
        sides = [pick(projections + j * width, width) for j in range(2)]
        more[0][...] = tile_weights(jnp.concatenate(sides, -1), inner)


def rows_norm(z_ref, n_ref):
    rows, count, _ = z_ref.shape
    for r in range(rows):
        n_ref[r * count : (r + 1) * count, :] = row_norm(z_ref[r])


def join_kernel(keep_ref, other_ref, z_ref, n_ref):
    half = keep_ref.shape[0]
    first = lax.axis_index("section") == 0
    z_ref[:half] = jnp.where(first, keep_ref[...], other_ref[...])
    z_ref[half:] = jnp.where(first, other_ref[...], keep_ref[...])
    rows_norm(z_ref, n_ref)


def out_project(t_ref, offsets, stride, z_ref, gate_ref, w_out, z1_ref, n_ref):
    rows, count, _ = z_ref.shape
    inner = w_out.shape[0]
    for r in range(rows):
        here = slice(r * count, (r + 1) * count)
        tri = t_ref[pl.ds(offsets[r], inner, stride=stride), :].astype(BF16)
        update = contract(tri, w_out, 0, 0)
        first = (z_ref[r].astype(F32) + gate_ref[here, :] * update).astype(BF16)
        z1_ref[here, :] = first
        n_ref[here, :] = row_norm(first)


def transition(in_ref, back_ref, n_ref, z1_ref, finish):
    trans, piece = back_ref.shape[0], 256
    for m in range(n_ref.shape[0] // STEP):
        here = slice(m * STEP, (m + 1) * STEP)
        normed = n_ref[here, :]
        acts = []
        for j in range(trans // piece):
            gate_w = in_ref[:, j * piece : (j + 1) * piece]
            up_w = in_ref[:, trans + j * piece : trans + (j + 1) * piece]
            gate = jnp.dot(normed, gate_w, preferred_element_type=F32)
            up = jnp.dot(normed, up_w, preferred_element_type=F32)
            acts.append((jax.nn.silu(gate) * up).astype(BF16))
        back = jnp.dot(jnp.concatenate(acts, -1), back_ref[...], preferred_element_type=F32)
        finish(m, (z1_ref[here, :].astype(F32) + back).astype(BF16))


def norm_kernel(inner, tri_ref, t_ref):
    count = t_ref.shape[1]
    for q in range(2):
        part = tri_ref[:, q].astype(F32)

        def mean(value):
            total = jnp.sum(value, 0)
            return (total + pltpu.roll(total, 4, 0)) * (1.0 / inner)

        centred = part - mean(part)[None]
        var = mean(centred * centred)
        normed = centred * lax.rsqrt(var + 1e-05)[None]
        t_ref[q * 4 * inner : (q + 1) * 4 * inner, :] = normed.reshape(4 * inner, count)


def update_kernel(
    inner,
    t_ref,
    z_ref,
    gate_ref,
    in_ref,
    back_ref,
    w_out_ref,
    turned_ref,
    masks_ref,
    owns_ref,
    lr_ref,
    keep_ref,
    send_ref,
    n_ref,
    z1_ref,
    o_ref,
):
    rows, count, width = z_ref.shape
    half = rows // 2
    offsets = [q * 4 * inner + r for q in range(2) for r in range(half)]
    out_project(t_ref, offsets, 4, z_ref, gate_ref, w_out_ref[...], z1_ref, n_ref)

    def finish(m, done):
        o_ref[m * STEP : (m + 1) * STEP, :] = done

    transition(in_ref, back_ref, n_ref, z1_ref, finish)
    owns = (owns_ref[:1, :] > 0.5)[None]
    full = o_ref[: half * count, :].reshape(half, count, width)
    short = o_ref[half * count :, :].reshape(half, count, width)
    keep_ref[...] = jnp.where(owns, full.astype(F32), short.astype(F32)).astype(BF16)
    send_ref[...] = jnp.where(owns, short.astype(F32), full.astype(F32)).astype(BF16)
    turned = turned_ref[...]
    normed = [row_norm(o_ref[r * count : (r + 1) * count, :]) for r in range(half)]
    put_tiles(
        turned, [normed[:2], normed[2:]], [masks_ref[0], masks_ref[1]], lr_ref, 0, inner
    )
    four = row_norm(
        jnp.concatenate(
            [o_ref[r * count : r * count + SHORT, :] for r in range(half, rows)], 0
        )
    )
    put_tiles(turned, [[four, jnp.zeros_like(four)]], [masks_ref[2]], lr_ref, 2, inner)


def last_kernel(
    inner,
    tri_ref,
    z_ref,
    gate_ref,
    in_ref,
    back_ref,
    w_out_ref,
    out_ref,
    t_ref,
    n_ref,
    z1_ref,
    o_ref,
    sems,
):
    rows, count, width = z_ref.shape
    copies = []

    def finish(m, done):
        part = pl.ds(m * (STEP // count), STEP // count)
        o_ref[m * (STEP // count) : (m + 1) * (STEP // count)] = done.reshape(-1, count, width)
        copies.append(pltpu.make_async_copy(o_ref.at[part], out_ref.at[part], sems.at[m]))
        copies[-1].start()

    t_ref[...] = layer_norm(tri_ref[...].reshape(inner, rows, count).astype(F32), 0).reshape(
        inner * rows, count
    )
    out_project(t_ref, range(rows), rows, z_ref, gate_ref, w_out_ref[...], z1_ref, n_ref)
    transition(in_ref, back_ref, n_ref, z1_ref, finish)
    for copy in copies:
        copy.wait()


def fast_body(pair, valid_tokens, crop_order, w_proj, w_out, w_in, w_back):
    _, rows, count, width = pair.shape
    devices = lax.axis_size("section") * lax.axis_size("row")
    inner, trans = w_out.shape[1], w_back.shape[1]
    swap = [(0, 1), (1, 0)]
    packed = 3 * trans + inner + w_proj.shape[2]

    vmem = pl.BlockSpec(memory_space=pltpu.VMEM)
    hbm = pl.BlockSpec(memory_space=pltpu.HBM)
    anywhere = pl.BlockSpec(memory_space=pl.ANY)
    shape = jax.ShapeDtypeStruct
    flat = pltpu.VMEM((rows * count, width), BF16)
    gates = shape((rows * count, width), F32)
    sems = pltpu.SemaphoreType.DMA

    def call(kernel, out_shape, n_in, scratch=(), out_specs=None, in_spec=vmem, cost=None):
        many = isinstance(out_shape, tuple)
        specs = out_specs or ((vmem,) * len(out_shape) if many else vmem)
        return pl.pallas_call(
            kernel,
            out_shape=out_shape,
            in_specs=[in_spec] * n_in if isinstance(n_in, int) else n_in,
            out_specs=specs,
            scratch_shapes=list(scratch),
            compiler_params=LIMIT,
            cost_estimate=cost,
        )

    def exchange(value):
        return lax.all_to_all(value, ("section", "row"), split_axis=0, concat_axis=0, tiled=True)

    inputs = [
        pltpu.with_memory_space_constraint(x, pltpu.HBM)
        for x in (crop_order, valid_tokens, pair, w_proj, w_in, w_back, w_out)
    ]
    scalars = [
        pltpu.SMEM(crop_order.shape, jnp.int32),
        pltpu.SMEM(valid_tokens.shape, jnp.int32),
        pltpu.VMEM(pair.shape, BF16),
    ]
    tokens = shape((rows * count, width), BF16)
    lr_shape = (devices, rows // 2 + 1, 8, count)
    lr = call(
        functools.partial(first_kernel, inner),
        shape(lr_shape, BF16),
        4,
        [pltpu.VMEM(lr_shape, BF16)]
        + scalars
        + [pltpu.VMEM(w_proj.shape[1:], BF16), sems((5 + rows // 4,))],
        out_specs=hbm,
        in_spec=hbm,
    )(*inputs[:4])
    light = pl.CostEstimate(flops=34 * 10**6, bytes_accessed=10**6, transcendentals=2 * 10**5)
    own, z, normed, owns, masks = call(
        stage_kernel,
        (
            shape((packed, width), BF16),
            shape((rows, count, width), BF16),
            tokens,
            shape((8, count), F32),
            shape((3, 8, count), F32),
        ),
        [hbm] * 7 + [anywhere],
        scalars + [sems((5 + (2 * trans + w_proj.shape[2]) // width,))],
        cost=light,
    )(*inputs, lr)

    sides = exchange(lr)
    other = lax.ppermute(own, "section", swap)
    readied = (
        gates,
        shape(w_in.shape[1:], BF16),
        shape(w_back.shape[1:], BF16),
        shape(w_out.shape[1:], BF16),
    )
    tri_scratch = [
        pltpu.VMEM((4 * count, count), F32),
        pltpu.VMEM((32, count), F32),
        pltpu.VMEM((CHANNELS, 32, count), F32),
    ]
    tri = exchange(
        call(
            first_triangle_kernel,
            shape((devices, 2, 8, count), BF16),
            [vmem, anywhere],
            tri_scratch,
        )(sides, normed),
    )
    t = call(functools.partial(norm_kernel, inner), shape((8 * inner, count), F32), 1)(tri)
    *ready, turned = call(
        functools.partial(ready_kernel, 0, inner, trans),
        readied + (shape((8 * inner, 2 * width), BF16),),
        [vmem, vmem, vmem, anywhere],
        cost=light,
    )(normed, own, other, t)
    work = [pltpu.VMEM((8 * inner, count), F32), flat, flat]
    halves = shape((rows // 2, count, width), BF16)
    lr, keep, send = call(
        functools.partial(update_kernel, inner),
        (shape((devices, 3, 8, count), BF16), halves, halves),
        9,
        [flat] * 3,
    )(t, z, *ready, turned, masks, owns)

    sides = exchange(lr)
    came = lax.ppermute(send, "section", swap)
    z, normed = call(join_kernel, (shape((rows, count, width), BF16), tokens), 2)(keep, came)
    ready = call(
        functools.partial(ready_kernel, 1, inner, trans), readied, [vmem, vmem, vmem, anywhere], cost=light
    )(normed, own, other, normed)
    tri_scratch[1] = pltpu.VMEM((64, count), F32)
    tri = exchange(
        call(
            last_triangle_kernel, shape((devices, CHANNELS, 8, count), BF16), 2, tri_scratch
        )(sides, owns),
    )
    out = call(
        functools.partial(last_kernel, inner),
        shape((rows, count, width), BF16),
        6,
        work + [pltpu.VMEM((rows, count, width), BF16), sems((rows * count // STEP,))],
        out_specs=hbm,
    )(tri, z, *ready)
    return out[None]


def pair_block(state, valid, row_start, w_proj, w_out, w_in, w_back):
    rows_here, count, width = state.shape
    inner, trans = w_out.shape[0], w_back.shape[0]
    normed = layer_norm(state.astype(F32)).astype(BF16).reshape(rows_here * count, width)
    proj = jnp.dot(normed, w_proj, preferred_element_type=F32).reshape(rows_here, count, -1)
    keep_cols = (jnp.arange(count) < valid).astype(F32)
    keep_rows = (row_start + jnp.arange(rows_here) < valid).astype(F32)
    mask = keep_rows[:, None, None] * keep_cols[None, :, None]
    left = (mask * jax.nn.sigmoid(proj[..., inner : 2 * inner]) * proj[..., :inner]).astype(BF16)
    right = (
        mask * jax.nn.sigmoid(proj[..., 3 * inner : 4 * inner]) * proj[..., 2 * inner : 3 * inner]
    ).astype(BF16)
    gate = jax.nn.sigmoid(proj[..., 4 * inner :])
    left_whole = lax.all_to_all(left, "row", split_axis=2, concat_axis=0, tiled=True)
    right_whole = lax.all_to_all(right, "row", split_axis=2, concat_axis=0, tiled=True)
    tri_part = jnp.einsum("ikc,jkc->ijc", left_whole, right_whole, preferred_element_type=F32)
    tri = lax.all_to_all(
        tri_part.astype(BF16), "row", split_axis=0, concat_axis=2, tiled=True
    ).astype(F32)
    tri_normed = layer_norm(tri).astype(BF16).reshape(rows_here * count, inner)
    update = jnp.dot(tri_normed, w_out, preferred_element_type=F32).reshape(rows_here, count, width)
    first = (state.astype(F32) + gate * update).astype(BF16)
    second = layer_norm(first.astype(F32)).astype(BF16).reshape(rows_here * count, width)
    hidden = jnp.dot(second, w_in, preferred_element_type=F32)
    act = (jax.nn.silu(hidden[:, :trans]) * hidden[:, trans:]).astype(BF16)
    back = jnp.dot(act, w_back, preferred_element_type=F32).reshape(rows_here, count, width)
    return (first.astype(F32) + back).astype(BF16)


def general_body(pair, valid_tokens, crop_order, w_proj, w_out, w_in, w_back):
    crops, rows_here = pair.shape[:2]
    row_start = lax.axis_index("row") * rows_here
    share = crops // lax.axis_size("section")
    section = lax.axis_index("section")
    weights = [
        lax.all_gather(w, "section", axis=0, tiled=True) for w in (w_proj, w_out, w_in, w_back)
    ]
    blocks = weights[0].shape[0]

    def one_crop(index, outputs):
        crop = crop_order[section * share + index]
        valid = valid_tokens[crop]
        state = lax.dynamic_index_in_dim(pair, crop, 0, keepdims=False)

        def apply_block(block, value):
            return pair_block(value, valid, row_start, *[w[block] for w in weights])

        final = lax.fori_loop(0, blocks, apply_block, state)
        return lax.dynamic_update_index_in_dim(outputs, final, index, 0)

    empty = jnp.zeros((share,) + pair.shape[1:], BF16)
    return lax.fori_loop(0, share, one_crop, empty)


def solution(mesh):
    sections, peers = mesh.shape["section"], mesh.shape["row"]

    def body(pair, valid_tokens, crop_order, w_proj, w_out, w_in, w_back):
        crops, rows, count, width = pair.shape
        inner, trans = w_out.shape[1], w_back.shape[1]
        fits = (
            sections == 2
            and crops == sections
            and w_proj.shape[0] == 1
            and rows == 8
            and count == width == 4 * SHORT
            and peers * rows == count
            and inner == 2 * CHANNELS * peers
            and w_proj.shape[2] == 3 * width
            and trans % 256 == 0
        )
        run = fast_body if fits else general_body
        return run(pair, valid_tokens, crop_order, w_proj, w_out, w_in, w_back)

    weights = P("section", None, None)
    return jax.shard_map(
        body,
        mesh=mesh,
        in_specs=(P(None, "row", None, None), P(), P(), weights, weights, weights, weights),
        out_specs=P("section", "row", None, None),
        check_vma=False,
    )
```

```python
import functools

import jax
import jax.numpy as jnp
from jax import lax
from jax.experimental import pallas as pl
from jax.experimental.pallas import tpu as pltpu
from jax.sharding import PartitionSpec as P


F32 = jnp.float32
BF16 = jnp.bfloat16
STEP = 512
CHANNELS = 2
SHORT = 32
LIMIT = pltpu.CompilerParams(vmem_limit_bytes=16 * 2**20)


def layer_norm(value, axis=-1):
    mean = jnp.mean(value, axis, keepdims=True)
    centred = value - mean
    var = jnp.mean(centred * centred, axis, keepdims=True)
    return centred * lax.rsqrt(var + 1e-05)


def row_norm(value):
    return layer_norm(value.astype(F32)).astype(BF16)


def contract(left, right, left_axis, right_axis):
    return lax.dot_general(
        left, right, (((left_axis,), (right_axis,)), ((), ())), preferred_element_type=F32
    )


def tile_weights(weights, inner):
    row = lax.broadcasted_iota(jnp.int32, (4 * inner, 2 * inner), 0)
    column = lax.broadcasted_iota(jnp.int32, (4 * inner, 2 * inner), 1)
    peer, slot = lax.div(row, 8), lax.rem(row, 4)
    source = lax.div(slot, 2) * inner + peer * CHANNELS + lax.rem(slot, 2)
    pick = jnp.where(column == source, 1.0, 0.0).astype(BF16)
    left, right = weights[:, : 2 * inner].astype(F32), weights[:, 2 * inner :].astype(F32)
    low = lax.broadcasted_iota(jnp.int32, left.shape, 1) < inner
    values = jnp.where(low, left, pltpu.roll(right, inner, 1)).astype(BF16)
    gates = jnp.where(low, pltpu.roll(left, inner, 1), right).astype(BF16)
    both = [contract(pick, part, 1, 1) for part in (values, gates)]
    half = lax.rem(lax.broadcasted_iota(jnp.int32, both[0].shape, 0), 8) < 4
    return jnp.concatenate(
        [
            jnp.concatenate([jnp.where(half, part, 0.0), jnp.where(half, 0.0, part)], -1)
            for part in both
        ],
        0,
    ).astype(BF16)


def put_tiles(turned, halves, masks, lr_ref, first, inner):
    peers, count = lr_ref.shape[0], lr_ref.shape[-1]
    normed = jnp.concatenate([jnp.concatenate(pair, -1) for pair in halves], 0)
    proj = contract(turned, normed, 1, 1)
    sides = jax.nn.sigmoid(proj[4 * inner :]) * proj[: 4 * inner]
    for i, mask in enumerate(masks):
        tile = sides[:, i * count : (i + 1) * count].reshape(peers, 8, count)
        lr_ref[:, first + i] = (tile * mask[None]).astype(BF16)


def full_mask(row, valid, count):
    half = lax.div(lax.broadcasted_iota(jnp.int32, (8, count), 0), 4)
    token = lax.broadcasted_iota(jnp.int32, (8, count), 1)
    return jnp.where(jnp.logical_and(row + half < valid, token < valid), 1.0, 0.0)


def short_mask(row, valid, count):
    half = lax.div(lax.broadcasted_iota(jnp.int32, (8, count), 0), 4)
    lane = lax.broadcasted_iota(jnp.int32, (8, count), 1)
    inside = row + 4 * half + lax.div(lane, SHORT) < valid
    return jnp.where(jnp.logical_and(inside, lax.rem(lane, SHORT) < valid), 1.0, 0.0)


def read_scalars(order_ref, valid_ref, order_s, valid_s, sems):
    copies = [
        pltpu.make_async_copy(order_ref, order_s, sems.at[0]),
        pltpu.make_async_copy(valid_ref, valid_s, sems.at[1]),
    ]
    for copy in copies:
        copy.start()
    return copies


def first_kernel(
    inner, order_ref, valid_ref, pair_ref, wp_ref, out_ref, lr_ref, order_s, valid_s, both_ref, w_ref, sems
):
    rows, count, width = pair_ref.shape[1:]
    copies = []

    def send(first, tiles):
        part = pl.ds(first, tiles)
        copies.append(
            pltpu.make_async_copy(lr_ref.at[:, part], out_ref.at[:, part], sems.at[4 + len(copies)])
        )
        copies[-1].start()

    @pl.when(lax.axis_index("section") == 0)
    def _():
        weights = pltpu.make_async_copy(wp_ref.at[0], w_ref, sems.at[2])
        weights.start()
        state = pltpu.make_async_copy(pair_ref, both_ref, sems.at[3])
        state.start()
        scalars = read_scalars(order_ref, valid_ref, order_s, valid_s, sems)
        weights.wait()
        turned = tile_weights(w_ref[:, : 4 * inner], inner)
        for copy in scalars:
            copy.wait()
        full = jnp.where(valid_s[1] > valid_s[0], 1, 0)
        short = 1 - full
        start = lax.axis_index("row") * rows
        state.wait()
        for t in range(0, rows // 2, 2):
            normed = [row_norm(both_ref[full, 2 * t + r]) for r in range(4)]
            put_tiles(
                turned,
                [normed[:2], normed[2:]],
                [full_mask(start + 2 * t + r, valid_s[full], count) for r in (0, 2)],
                lr_ref,
                t,
                inner,
            )
            send(t, 2)
        fours = [
            row_norm(both_ref[short, 4 * h : 4 * h + 4, :SHORT].reshape(4 * SHORT, width))
            for h in range(2)
        ]
        put_tiles(
            turned, [fours], [short_mask(start, valid_s[short], count)], lr_ref, rows // 2, inner
        )
        send(rows // 2, 1)
        for copy in copies:
            copy.wait()


def pack(sources, target_ref, sems, first):
    copies, at = [], 0
    for i, source in enumerate(sources):
        part = target_ref.at[pl.ds(at, source.shape[0])]
        copies.append(pltpu.make_async_copy(source, part, sems.at[first + i]))
        copies[-1].start()
        at += source.shape[0]
    return copies


def small_kernel(wp_ref, w_out_ref, after_ref, small_ref, sems):
    width = small_ref.shape[1]
    sources = [wp_ref.at[0, :, pl.ds(j * width, width)] for j in range(wp_ref.shape[2] // width)]
    for copy in pack(sources + [w_out_ref.at[0]], small_ref, sems, 0):
        copy.wait()


def stage_kernel(
    order_ref,
    valid_ref,
    pair_ref,
    w_in_ref,
    w_back_ref,
    after_ref,
    large_ref,
    z_ref,
    n_ref,
    owns_ref,
    masks_ref,
    order_s,
    valid_s,
    both_ref,
    sems,
):
    rows, count, width = z_ref.shape
    trans = w_back_ref.shape[1]
    sources = [w_in_ref.at[0, :, pl.ds(j * width, width)] for j in range(2 * trans // width)]
    packing = pack(sources + [w_back_ref.at[0]], large_ref, sems, 3)
    scalars = read_scalars(order_ref, valid_ref, order_s, valid_s, sems)
    state = pltpu.make_async_copy(pair_ref, both_ref, sems.at[2])
    state.start()
    for copy in scalars:
        copy.wait()
    section = lax.axis_index("section")
    full = jnp.where(valid_s[1] > valid_s[0], 1, 0)
    short = 1 - full
    owns_ref[...] = jnp.full(owns_ref.shape, jnp.where(order_s[section] == full, 1.0, 0.0))
    mine = lax.axis_index("row") * rows + (rows // 2) * section
    masks_ref[0] = full_mask(mine, valid_s[full], count)
    masks_ref[1] = full_mask(mine + 2, valid_s[full], count)
    masks_ref[2] = short_mask(mine, valid_s[short], count)
    state.wait()
    half = pl.ds((rows // 2) * section, rows // 2)
    z_ref[: rows // 2] = both_ref[full, half]
    z_ref[rows // 2 :] = both_ref[short, half]
    rows_norm(z_ref, n_ref)
    for copy in packing:
        copy.wait()


def short_triangle(left, right, place_ref):
    count = left.shape[1]
    block = lax.div(lax.broadcasted_iota(jnp.int32, left.shape, 1), SHORT)
    lefts = jnp.concatenate([jnp.where(block == q, left, 0.0) for q in range(4)], 0)
    rights = jnp.concatenate(
        [right if q == 0 else pltpu.roll(right, SHORT * q, 1) for q in range(4)], 0
    )
    product = contract(lefts.astype(BF16), rights.astype(BF16), 1, 1).astype(BF16)
    source = lax.broadcasted_iota(jnp.int32, (32, count), 0)
    target = lax.broadcasted_iota(jnp.int32, (32, count), 1)
    moved, token = lax.div(source, 8), lax.rem(source, 8)
    for q in range(4):
        lane = 4 * token + lax.rem(q - moved + 4, 4)
        pick = jnp.where(target == lane, 1.0, 0.0).astype(BF16)
        place_ref[pl.ds(q, 8, stride=4), :] = jnp.dot(
            product[8 * q : 8 * q + 8], pick, preferred_element_type=F32
        )


def triangles(wide_ref, few_ref, few_stride, place_ref, count):
    results = []
    for c in range(CHANNELS):
        left = wide_ref[pl.ds(c, count, stride=4), :].astype(BF16)
        right = wide_ref[pl.ds(2 + c, count, stride=4), :].astype(BF16)
        short_triangle(
            few_ref[pl.ds(c, 8, stride=few_stride), :],
            few_ref[pl.ds(2 + c, 8, stride=few_stride), :],
            place_ref.at[c],
        )
        results.append((contract(left, right, 1, 1), place_ref[c]))
    return results


def first_triangle_kernel(in_ref, after_ref, out_ref, wide_ref, few_ref, place_ref):
    peers, count = in_ref.shape[0], in_ref.shape[-1]
    rows = peers // 2
    tiles = in_ref.shape[1] - 1
    wide_ref[...] = in_ref[:rows, :tiles].astype(F32).reshape(rows * tiles * 8, count)
    few_ref[...] = in_ref[:4, tiles].astype(F32).reshape(32, count)
    results = triangles(wide_ref, few_ref, 4, place_ref, count)
    for q in range(2):
        one, two = [r[q].reshape(-1, 8, count) for r in results]
        low = lax.broadcasted_iota(jnp.int32, one.shape, 1) < 4
        groups = one.shape[0]
        tiles = (
            jnp.where(low, one, pltpu.roll(two, 4, 1)),
            jnp.where(low, pltpu.roll(one, 4, 1), two),
        )
        for section, tile in enumerate(tiles):
            out_ref[section * rows : section * rows + groups, q] = tile.astype(BF16)
            if groups < rows:
                out_ref[section * rows + groups : (section + 1) * rows, q] = jnp.zeros(
                    (rows - groups, 8, count), BF16
                )


def last_triangle_kernel(in_ref, owns_ref, out_ref, wide_ref, few_ref, place_ref):
    peers, count = in_ref.shape[0], in_ref.shape[-1]
    rows = peers // 2
    for r in range(rows):
        for section in range(2):
            at = 2 * r + section
            tiles = in_ref[section * rows + r]
            wide_ref[16 * at : 16 * at + 16, :] = tiles[:2].astype(F32).reshape(16, count)
            if at < 8:
                few_ref[8 * at : 8 * at + 8, :] = tiles[2].astype(F32)
    zero_owns = jnp.where(lax.axis_index("section") == 0, owns_ref[...], 1.0 - owns_ref[...]) > 0.5
    results = triangles(wide_ref, few_ref, 8, place_ref, count)
    for c, (full, short) in enumerate(results):
        full = full.reshape(rows, 8, count)
        short = short.reshape(-1, 8, count)
        groups = short.shape[0]
        for section in range(2):
            is_full = zero_owns if section == 0 else jnp.logical_not(zero_owns)
            at = section * rows
            out_ref[at : at + groups, c] = jnp.where(is_full[None], full[:groups], short).astype(BF16)
            out_ref[at + groups : at + rows, c] = jnp.where(
                is_full[None], full[groups:], 0.0
            ).astype(BF16)


def picker(block, own_ref, other_ref):
    mine = lax.axis_index("section") == block

    def pick(start, size):
        here = slice(start, start + size)
        return jnp.where(mine, own_ref[here, :], other_ref[here, :])

    return pick


def gates_and_sides(block, inner, n_ref, own_ref, other_ref, gate_ref, w_out_ref, turned_ref=None):
    width = n_ref.shape[1]
    pick = picker(block, own_ref, other_ref)
    weights = pick(2 * width, width)
    step = 512
    for m in range(n_ref.shape[0] // step):
        here = slice(m * step, (m + 1) * step)
        gate_ref[here, :] = jax.nn.sigmoid(
            jnp.dot(n_ref[here, :], weights, preferred_element_type=F32)
        )
    w_out_ref[...] = pick(3 * width, inner)
    if turned_ref is not None:
        pick = picker(block + 1, own_ref, other_ref)
        sides = [pick(j * width, width) for j in range(2)]
        turned_ref[...] = tile_weights(jnp.concatenate(sides, -1), inner)


def transition_weights(block, own_ref, other_ref, in_ref, back_ref):
    width, hidden = in_ref.shape
    pick = picker(block, own_ref, other_ref)
    for j in range(hidden // width):
        in_ref[:, j * width : (j + 1) * width] = pick(j * width, width)
    back_ref[...] = pick(hidden, back_ref.shape[0])


def ready_last_kernel(
    inner, n_ref, own_ref, other_ref, large_ref, other_large_ref, gate_ref, w_out_ref, in_ref, back_ref
):
    gates_and_sides(1, inner, n_ref, own_ref, other_ref, gate_ref, w_out_ref)
    transition_weights(1, large_ref, other_large_ref, in_ref, back_ref)


def rows_norm(z_ref, n_ref):
    rows, count, _ = z_ref.shape
    for r in range(rows):
        n_ref[r * count : (r + 1) * count, :] = row_norm(z_ref[r])


def join_kernel(keep_ref, other_ref, z_ref, n_ref):
    half = keep_ref.shape[0]
    first = lax.axis_index("section") == 0
    z_ref[:half] = jnp.where(first, keep_ref[...], other_ref[...])
    z_ref[half:] = jnp.where(first, other_ref[...], keep_ref[...])
    rows_norm(z_ref, n_ref)


def out_project(which, t_ref, offsets, stride, z_ref, gate_ref, w_out, z1_ref, n_ref):
    _, count, _ = z_ref.shape
    inner = w_out.shape[0]
    for r in which:
        here = slice(r * count, (r + 1) * count)
        tri = t_ref[pl.ds(offsets[r], inner, stride=stride), :].astype(BF16)
        update = contract(tri, w_out, 0, 0)
        first = (z_ref[r].astype(F32) + gate_ref[here, :] * update).astype(BF16)
        z1_ref[here, :] = first
        n_ref[here, :] = row_norm(first)


def transition(which, in_ref, back_ref, n_ref, z1_ref, finish):
    trans, piece = back_ref.shape[0], 256
    for m in which:
        here = slice(m * STEP, (m + 1) * STEP)
        normed = n_ref[here, :]
        acts = []
        for j in range(trans // piece):
            gate_w = in_ref[:, j * piece : (j + 1) * piece]
            up_w = in_ref[:, trans + j * piece : trans + (j + 1) * piece]
            gate = jnp.dot(normed, gate_w, preferred_element_type=F32)
            up = jnp.dot(normed, up_w, preferred_element_type=F32)
            acts.append((jax.nn.silu(gate) * up).astype(BF16))
        back = jnp.dot(jnp.concatenate(acts, -1), back_ref[...], preferred_element_type=F32)
        finish(m, (z1_ref[here, :].astype(F32) + back).astype(BF16))


def norm_kernel(inner, tri_ref, t_ref):
    count = t_ref.shape[1]
    for q in range(2):
        part = tri_ref[:, q].astype(F32)

        def mean(value):
            total = jnp.sum(value, 0)
            return (total + pltpu.roll(total, 4, 0)) * (1.0 / inner)

        centred = part - mean(part)[None]
        var = mean(centred * centred)
        normed = centred * lax.rsqrt(var + 1e-05)[None]
        t_ref[q * 4 * inner : (q + 1) * 4 * inner, :] = normed.reshape(4 * inner, count)


def update_kernel(
    inner,
    t_ref,
    z_ref,
    gate_ref,
    w_out_ref,
    turned_ref,
    large_ref,
    other_large_ref,
    masks_ref,
    owns_ref,
    lr_ref,
    keep_ref,
    send_ref,
    n_ref,
    z1_ref,
    o_ref,
    in_ref,
    back_ref,
):
    rows, count, width = z_ref.shape
    half = rows // 2
    transition_weights(0, large_ref, other_large_ref, in_ref, back_ref)
    offsets = [q * 4 * inner + r for q in range(2) for r in range(half)]
    project = functools.partial(
        out_project,
        t_ref=t_ref,
        offsets=offsets,
        stride=4,
        z_ref=z_ref,
        gate_ref=gate_ref,
        w_out=w_out_ref[...],
        z1_ref=z1_ref,
        n_ref=n_ref,
    )

    def finish(m, done):
        o_ref[m * STEP : (m + 1) * STEP, :] = done

    turned = turned_ref[...]

    def tail_full():
        normed = [row_norm(o_ref[r * count : (r + 1) * count, :]) for r in range(half)]
        put_tiles(
            turned, [normed[:2], normed[2:]], [masks_ref[0], masks_ref[1]], lr_ref, 0, inner
        )

    project(range(rows))
    transition((0, 1), in_ref, back_ref, n_ref, z1_ref, finish)
    tail_full()
    owns = (owns_ref[:1, :] > 0.5)[None]
    full = o_ref[: half * count, :].reshape(half, count, width)
    short = o_ref[half * count :, :].reshape(half, count, width)
    keep_ref[...] = jnp.where(owns, full.astype(F32), short.astype(F32)).astype(BF16)
    send_ref[...] = jnp.where(owns, short.astype(F32), full.astype(F32)).astype(BF16)
    four = row_norm(
        jnp.concatenate(
            [o_ref[r * count : r * count + SHORT, :] for r in range(half, rows)], 0
        )
    )
    put_tiles(turned, [[four, jnp.zeros_like(four)]], [masks_ref[2]], lr_ref, 2, inner)


def last_kernel(
    inner,
    tri_ref,
    z_ref,
    gate_ref,
    w_out_ref,
    in_ref,
    back_ref,
    out_ref,
    t_ref,
    n_ref,
    z1_ref,
    o_ref,
    sems,
):
    rows, count, width = z_ref.shape
    copies = []

    def finish(m, done):
        part = pl.ds(m * (STEP // count), STEP // count)
        o_ref[m * (STEP // count) : (m + 1) * (STEP // count)] = done.reshape(-1, count, width)
        copies.append(pltpu.make_async_copy(o_ref.at[part], out_ref.at[part], sems.at[m]))
        copies[-1].start()

    t_ref[...] = layer_norm(tri_ref[...].reshape(inner, rows, count).astype(F32), 0).reshape(
        inner * rows, count
    )
    args = (t_ref, range(rows), rows, z_ref, gate_ref, w_out_ref[...], z1_ref, n_ref)
    out_project(range(rows), *args)
    transition((0, 1), in_ref, back_ref, n_ref, z1_ref, finish)
    for copy in copies:
        copy.wait()


def fast_body(pair, valid_tokens, crop_order, w_proj, w_out, w_in, w_back):
    _, rows, count, width = pair.shape
    devices = lax.axis_size("section") * lax.axis_size("row")
    inner, trans = w_out.shape[1], w_back.shape[1]
    swap = [(0, 1), (1, 0)]

    vmem = pl.BlockSpec(memory_space=pltpu.VMEM)
    hbm = pl.BlockSpec(memory_space=pltpu.HBM)
    anywhere = pl.BlockSpec(memory_space=pl.ANY)
    shape = jax.ShapeDtypeStruct
    flat = pltpu.VMEM((rows * count, width), BF16)
    gates = shape((rows * count, width), F32)
    sems = pltpu.SemaphoreType.DMA

    def call(
        kernel, out_shape, n_in, scratch=(), out_specs=None, in_spec=vmem, cost=None, params=LIMIT
    ):
        many = isinstance(out_shape, tuple)
        specs = out_specs or ((vmem,) * len(out_shape) if many else vmem)
        return pl.pallas_call(
            kernel,
            out_shape=out_shape,
            in_specs=[in_spec] * n_in if isinstance(n_in, int) else n_in,
            out_specs=specs,
            scratch_shapes=list(scratch),
            compiler_params=params,
            cost_estimate=cost,
        )

    def exchange(value):
        return lax.all_to_all(value, ("section", "row"), split_axis=0, concat_axis=0, tiled=True)

    inputs = [
        pltpu.with_memory_space_constraint(x, pltpu.HBM)
        for x in (crop_order, valid_tokens, pair, w_proj, w_in, w_back, w_out)
    ]
    scalars = [
        pltpu.SMEM(crop_order.shape, jnp.int32),
        pltpu.SMEM(valid_tokens.shape, jnp.int32),
        pltpu.VMEM(pair.shape, BF16),
    ]
    tokens = shape((rows * count, width), BF16)
    lr_shape = (devices, rows // 2 + 1, 8, count)
    lr = call(
        functools.partial(first_kernel, inner),
        shape(lr_shape, BF16),
        4,
        [pltpu.VMEM(lr_shape, BF16)]
        + scalars
        + [pltpu.VMEM(w_proj.shape[1:], BF16), sems((5 + rows // 4,))],
        out_specs=hbm,
        in_spec=hbm,
    )(*inputs[:4])
    light = pl.CostEstimate(flops=34 * 10**6, bytes_accessed=10**6, transcendentals=2 * 10**5)
    small = call(
        small_kernel,
        shape((w_proj.shape[2] + inner, width), BF16),
        [hbm] * 2 + [anywhere],
        [sems((1 + w_proj.shape[2] // width,))],
        cost=light,
    )(inputs[3], inputs[6], lr)
    large, z, normed, owns, masks = call(
        stage_kernel,
        (
            shape((3 * trans, width), BF16),
            shape((rows, count, width), BF16),
            tokens,
            shape((8, count), F32),
            shape((3, 8, count), F32),
        ),
        [hbm] * 5 + [anywhere],
        scalars + [sems((4 + 2 * trans // width,))],
        cost=light,
    )(*inputs[:3], *inputs[4:6], small)

    sides = exchange(lr)
    other_small = lax.ppermute(small, "section", swap)
    other_large = lax.ppermute(large, "section", swap)
    gate, w_out_first, turned = call(
        functools.partial(gates_and_sides, 0, inner),
        (gates, shape(w_out.shape[1:], BF16), shape((8 * inner, 2 * width), BF16)),
        3,
        cost=light,
    )(normed, small, other_small)
    tri_scratch = [
        pltpu.VMEM((4 * count, count), F32),
        pltpu.VMEM((32, count), F32),
        pltpu.VMEM((CHANNELS, 32, count), F32),
    ]
    tri = exchange(
        call(
            first_triangle_kernel,
            shape((devices, 2, 8, count), BF16),
            [vmem, anywhere],
            tri_scratch,
        )(sides, gate),
    )
    t = call(functools.partial(norm_kernel, inner), shape((8 * inner, count), F32), 1)(tri)
    work = [pltpu.VMEM((8 * inner, count), F32), flat, flat]
    halves = shape((rows // 2, count, width), BF16)
    lr, keep, send = call(
        functools.partial(update_kernel, inner),
        (shape((devices, 3, 8, count), BF16), halves, halves),
        9,
        [flat] * 3 + [pltpu.VMEM(w_in.shape[1:], BF16), pltpu.VMEM(w_back.shape[1:], BF16)],
    )(t, z, gate, w_out_first, turned, large, other_large, masks, owns)

    sides = exchange(lr)
    came = lax.ppermute(send, "section", swap)
    z, normed = call(join_kernel, (shape((rows, count, width), BF16), tokens), 2)(keep, came)
    ready = call(
        functools.partial(ready_last_kernel, inner),
        tuple(shape(x, BF16 if i else F32) for i, x in enumerate(
            ((rows * count, width), w_out.shape[1:], w_in.shape[1:], w_back.shape[1:])
        )),
        5,
        cost=light,
    )(normed, small, other_small, large, other_large)
    tri_scratch[1] = pltpu.VMEM((64, count), F32)
    tri = exchange(
        call(
            last_triangle_kernel, shape((devices, CHANNELS, 8, count), BF16), 2, tri_scratch
        )(sides, owns),
    )
    out = call(
        functools.partial(last_kernel, inner),
        shape((rows, count, width), BF16),
        6,
        work + [pltpu.VMEM((rows, count, width), BF16), sems((rows * count // STEP,))],
        out_specs=hbm,
    )(tri, z, *ready)
    return out[None]


def pair_block(state, valid, row_start, w_proj, w_out, w_in, w_back):
    rows_here, count, width = state.shape
    inner, trans = w_out.shape[0], w_back.shape[0]
    normed = layer_norm(state.astype(F32)).astype(BF16).reshape(rows_here * count, width)
    proj = jnp.dot(normed, w_proj, preferred_element_type=F32).reshape(rows_here, count, -1)
    keep_cols = (jnp.arange(count) < valid).astype(F32)
    keep_rows = (row_start + jnp.arange(rows_here) < valid).astype(F32)
    mask = keep_rows[:, None, None] * keep_cols[None, :, None]
    left = (mask * jax.nn.sigmoid(proj[..., inner : 2 * inner]) * proj[..., :inner]).astype(BF16)
    right = (
        mask * jax.nn.sigmoid(proj[..., 3 * inner : 4 * inner]) * proj[..., 2 * inner : 3 * inner]
    ).astype(BF16)
    gate = jax.nn.sigmoid(proj[..., 4 * inner :])
    left_whole = lax.all_to_all(left, "row", split_axis=2, concat_axis=0, tiled=True)
    right_whole = lax.all_to_all(right, "row", split_axis=2, concat_axis=0, tiled=True)
    tri_part = jnp.einsum("ikc,jkc->ijc", left_whole, right_whole, preferred_element_type=F32)
    tri = lax.all_to_all(
        tri_part.astype(BF16), "row", split_axis=0, concat_axis=2, tiled=True
    ).astype(F32)
    tri_normed = layer_norm(tri).astype(BF16).reshape(rows_here * count, inner)
    update = jnp.dot(tri_normed, w_out, preferred_element_type=F32).reshape(rows_here, count, width)
    first = (state.astype(F32) + gate * update).astype(BF16)
    second = layer_norm(first.astype(F32)).astype(BF16).reshape(rows_here * count, width)
    hidden = jnp.dot(second, w_in, preferred_element_type=F32)
    act = (jax.nn.silu(hidden[:, :trans]) * hidden[:, trans:]).astype(BF16)
    back = jnp.dot(act, w_back, preferred_element_type=F32).reshape(rows_here, count, width)
    return (first.astype(F32) + back).astype(BF16)


def general_body(pair, valid_tokens, crop_order, w_proj, w_out, w_in, w_back):
    crops, rows_here = pair.shape[:2]
    row_start = lax.axis_index("row") * rows_here
    share = crops // lax.axis_size("section")
    section = lax.axis_index("section")
    weights = [
        lax.all_gather(w, "section", axis=0, tiled=True) for w in (w_proj, w_out, w_in, w_back)
    ]
    blocks = weights[0].shape[0]

    def one_crop(index, outputs):
        crop = crop_order[section * share + index]
        valid = valid_tokens[crop]
        state = lax.dynamic_index_in_dim(pair, crop, 0, keepdims=False)

        def apply_block(block, value):
            return pair_block(value, valid, row_start, *[w[block] for w in weights])

        final = lax.fori_loop(0, blocks, apply_block, state)
        return lax.dynamic_update_index_in_dim(outputs, final, index, 0)

    empty = jnp.zeros((share,) + pair.shape[1:], BF16)
    return lax.fori_loop(0, share, one_crop, empty)


def solution(mesh):
    sections, peers = mesh.shape["section"], mesh.shape["row"]

    def body(pair, valid_tokens, crop_order, w_proj, w_out, w_in, w_back):
        crops, rows, count, width = pair.shape
        inner, trans = w_out.shape[1], w_back.shape[1]
        fits = (
            sections == 2
            and crops == sections
            and w_proj.shape[0] == 1
            and rows == 8
            and count == width == 4 * SHORT
            and peers * rows == count
            and inner == 2 * CHANNELS * peers
            and w_proj.shape[2] == 3 * width
            and trans % 256 == 0
        )
        run = fast_body if fits else general_body
        return run(pair, valid_tokens, crop_order, w_proj, w_out, w_in, w_back)

    weights = P("section", None, None)
    return jax.shard_map(
        body,
        mesh=mesh,
        in_specs=(P(None, "row", None, None), P(), P(), weights, weights, weights, weights),
        out_specs=P("section", "row", None, None),
        check_vma=False,
    )
```

```python
import functools

import jax
import jax.numpy as jnp
from jax import lax
from jax.experimental import pallas as pl
from jax.experimental.pallas import tpu as pltpu
from jax.sharding import PartitionSpec as P


F32 = jnp.float32
BF16 = jnp.bfloat16
STEP = 512
CHANNELS = 2
SHORT = 32
LIMIT = pltpu.CompilerParams(vmem_limit_bytes=16 * 2**20)


def layer_norm(value, axis=-1):
    mean = jnp.mean(value, axis, keepdims=True)
    centred = value - mean
    var = jnp.mean(centred * centred, axis, keepdims=True)
    return centred * lax.rsqrt(var + 1e-05)


def row_norm(value):
    return layer_norm(value.astype(F32)).astype(BF16)


def contract(left, right, left_axis, right_axis):
    return lax.dot_general(
        left, right, (((left_axis,), (right_axis,)), ((), ())), preferred_element_type=F32
    )


def tile_weights(weights, inner):
    row = lax.broadcasted_iota(jnp.int32, (4 * inner, 2 * inner), 0)
    column = lax.broadcasted_iota(jnp.int32, (4 * inner, 2 * inner), 1)
    peer, slot = lax.div(row, 8), lax.rem(row, 4)
    source = lax.div(slot, 2) * inner + peer * CHANNELS + lax.rem(slot, 2)
    pick = jnp.where(column == source, 1.0, 0.0).astype(BF16)
    left, right = weights[:, : 2 * inner].astype(F32), weights[:, 2 * inner :].astype(F32)
    low = lax.broadcasted_iota(jnp.int32, left.shape, 1) < inner
    values = jnp.where(low, left, pltpu.roll(right, inner, 1)).astype(BF16)
    gates = jnp.where(low, pltpu.roll(left, inner, 1), right).astype(BF16)
    both = [contract(pick, part, 1, 1) for part in (values, gates)]
    half = lax.rem(lax.broadcasted_iota(jnp.int32, both[0].shape, 0), 8) < 4
    return jnp.concatenate(
        [
            jnp.concatenate([jnp.where(half, part, 0.0), jnp.where(half, 0.0, part)], -1)
            for part in both
        ],
        0,
    ).astype(BF16)


def put_tiles(turned, halves, masks, lr_ref, first, inner):
    peers, count = lr_ref.shape[0], lr_ref.shape[-1]
    normed = jnp.concatenate([jnp.concatenate(pair, -1) for pair in halves], 0)
    proj = contract(turned, normed, 1, 1)
    sides = jax.nn.sigmoid(proj[4 * inner :]) * proj[: 4 * inner]
    for i, mask in enumerate(masks):
        tile = sides[:, i * count : (i + 1) * count].reshape(peers, 8, count)
        lr_ref[:, first + i] = (tile * mask[None]).astype(BF16)


def full_mask(row, valid, count):
    half = lax.div(lax.broadcasted_iota(jnp.int32, (8, count), 0), 4)
    token = lax.broadcasted_iota(jnp.int32, (8, count), 1)
    return jnp.where(jnp.logical_and(row + half < valid, token < valid), 1.0, 0.0)


def short_mask(row, valid, count):
    half = lax.div(lax.broadcasted_iota(jnp.int32, (8, count), 0), 4)
    lane = lax.broadcasted_iota(jnp.int32, (8, count), 1)
    inside = row + 4 * half + lax.div(lane, SHORT) < valid
    return jnp.where(jnp.logical_and(inside, lax.rem(lane, SHORT) < valid), 1.0, 0.0)


def read_scalars(order_ref, valid_ref, order_s, valid_s, sems):
    copies = [
        pltpu.make_async_copy(order_ref, order_s, sems.at[0]),
        pltpu.make_async_copy(valid_ref, valid_s, sems.at[1]),
    ]
    for copy in copies:
        copy.start()
    return copies


def first_kernel(
    inner, order_ref, valid_ref, pair_ref, wp_ref, out_ref, lr_ref, order_s, valid_s, both_ref, w_ref, sems
):
    rows, count, width = pair_ref.shape[1:]
    copies = []

    def send(first, tiles):
        part = pl.ds(first, tiles)
        copies.append(
            pltpu.make_async_copy(lr_ref.at[:, part], out_ref.at[:, part], sems.at[4 + len(copies)])
        )
        copies[-1].start()

    @pl.when(lax.axis_index("section") == 0)
    def _():
        weights = pltpu.make_async_copy(wp_ref.at[0], w_ref, sems.at[2])
        weights.start()
        state = pltpu.make_async_copy(pair_ref, both_ref, sems.at[3])
        state.start()
        scalars = read_scalars(order_ref, valid_ref, order_s, valid_s, sems)
        for copy in scalars:
            copy.wait()
        full = jnp.where(valid_s[1] > valid_s[0], 1, 0)
        short = 1 - full
        start = lax.axis_index("row") * rows
        weights.wait()
        state.wait()
        turned = tile_weights(w_ref[:, : 4 * inner], inner)
        for t in range(0, rows // 2, 2):
            normed = [row_norm(both_ref[full, 2 * t + r]) for r in range(4)]
            put_tiles(
                turned,
                [normed[:2], normed[2:]],
                [full_mask(start + 2 * t + r, valid_s[full], count) for r in (0, 2)],
                lr_ref,
                t,
                inner,
            )
            send(t, 2)
        fours = [
            row_norm(both_ref[short, 4 * h : 4 * h + 4, :SHORT].reshape(4 * SHORT, width))
            for h in range(2)
        ]
        put_tiles(
            turned, [fours], [short_mask(start, valid_s[short], count)], lr_ref, rows // 2, inner
        )
        send(rows // 2, 1)
        for copy in copies:
            copy.wait()


def pack(sources, target_ref, sems, first):
    copies, at = [], 0
    for i, source in enumerate(sources):
        part = target_ref.at[pl.ds(at, source.shape[0])]
        copies.append(pltpu.make_async_copy(source, part, sems.at[first + i]))
        copies[-1].start()
        at += source.shape[0]
    return copies


def small_kernel(wp_ref, w_out_ref, after_ref, small_ref, sems):
    width = small_ref.shape[1]
    sources = [wp_ref.at[0, :, pl.ds(j * width, width)] for j in range(wp_ref.shape[2] // width)]
    for copy in pack(sources + [w_out_ref.at[0]], small_ref, sems, 0):
        copy.wait()


def stage_kernel(
    order_ref,
    valid_ref,
    pair_ref,
    w_in_ref,
    w_back_ref,
    after_ref,
    large_ref,
    z_ref,
    n_ref,
    owns_ref,
    masks_ref,
    order_s,
    valid_s,
    both_ref,
    sems,
):
    rows, count, width = z_ref.shape
    trans = w_back_ref.shape[1]
    sources = [w_in_ref.at[0, :, pl.ds(j * width, width)] for j in range(2 * trans // width)]
    packing = pack(sources + [w_back_ref.at[0]], large_ref, sems, 3)
    scalars = read_scalars(order_ref, valid_ref, order_s, valid_s, sems)
    state = pltpu.make_async_copy(pair_ref, both_ref, sems.at[2])
    state.start()
    for copy in scalars:
        copy.wait()
    section = lax.axis_index("section")
    full = jnp.where(valid_s[1] > valid_s[0], 1, 0)
    short = 1 - full
    owns_ref[...] = jnp.full(owns_ref.shape, jnp.where(order_s[section] == full, 1.0, 0.0))
    mine = lax.axis_index("row") * rows + (rows // 2) * section
    masks_ref[0] = full_mask(mine, valid_s[full], count)
    masks_ref[1] = full_mask(mine + 2, valid_s[full], count)
    masks_ref[2] = short_mask(mine, valid_s[short], count)
    state.wait()
    half = pl.ds((rows // 2) * section, rows // 2)
    z_ref[: rows // 2] = both_ref[full, half]
    z_ref[rows // 2 :] = both_ref[short, half]
    rows_norm(z_ref, n_ref)
    for copy in packing:
        copy.wait()


def short_triangle(left, right, place_ref):
    count = left.shape[1]
    block = lax.div(lax.broadcasted_iota(jnp.int32, left.shape, 1), SHORT)
    lefts = jnp.concatenate([jnp.where(block == q, left, 0.0) for q in range(4)], 0)
    turned = [right if q == 0 else pltpu.roll(right, SHORT * q, 1) for q in range(4)]
    rights = jnp.concatenate(turned * 4, 0)
    product = contract(lefts.astype(BF16), rights.astype(BF16), 1, 1)
    row = lax.div(lax.broadcasted_iota(jnp.int32, product.shape, 0), 8)
    group = lax.div(lax.broadcasted_iota(jnp.int32, product.shape, 1), SHORT)
    product = jnp.where(row == group, product, 0.0).astype(BF16)
    source = lax.broadcasted_iota(jnp.int32, (count, count), 0)
    target = lax.broadcasted_iota(jnp.int32, (count, count), 1)
    moved, token = lax.rem(lax.div(source, 8), 4), lax.rem(source, 8)
    lane = 4 * token + lax.rem(lax.div(source, SHORT) - moved + 4, 4)
    pick = jnp.where(target == lane, 1.0, 0.0).astype(BF16)
    placed = jnp.dot(product, pick, preferred_element_type=F32)
    for q in range(4):
        place_ref[pl.ds(q, 8, stride=4), :] = placed[8 * q : 8 * q + 8]


def triangles(wide_ref, few_ref, few_stride, place_ref, count):
    results = []
    for c in range(CHANNELS):
        left = wide_ref[pl.ds(c, count, stride=4), :].astype(BF16)
        right = wide_ref[pl.ds(2 + c, count, stride=4), :].astype(BF16)
        short_triangle(
            few_ref[pl.ds(c, 8, stride=few_stride), :],
            few_ref[pl.ds(2 + c, 8, stride=few_stride), :],
            place_ref.at[c],
        )
        results.append((contract(left, right, 1, 1), place_ref[c]))
    return results


def first_triangle_kernel(in_ref, after_ref, out_ref, wide_ref, few_ref, place_ref):
    peers, count = in_ref.shape[0], in_ref.shape[-1]
    rows = peers // 2
    tiles = in_ref.shape[1] - 1
    wide_ref[...] = in_ref[:rows, :tiles].astype(F32).reshape(rows * tiles * 8, count)
    few_ref[...] = in_ref[:4, tiles].astype(F32).reshape(32, count)
    results = triangles(wide_ref, few_ref, 4, place_ref, count)
    for q in range(2):
        one, two = [r[q].reshape(-1, 8, count) for r in results]
        low = lax.broadcasted_iota(jnp.int32, one.shape, 1) < 4
        groups = one.shape[0]
        tiles = (
            jnp.where(low, one, pltpu.roll(two, 4, 1)),
            jnp.where(low, pltpu.roll(one, 4, 1), two),
        )
        for section, tile in enumerate(tiles):
            out_ref[section * rows : section * rows + groups, q] = tile.astype(BF16)
            if groups < rows:
                out_ref[section * rows + groups : (section + 1) * rows, q] = jnp.zeros(
                    (rows - groups, 8, count), BF16
                )


def last_triangle_kernel(in_ref, owns_ref, out_ref, wide_ref, few_ref, place_ref):
    peers, count = in_ref.shape[0], in_ref.shape[-1]
    rows = peers // 2
    for r in range(rows):
        for section in range(2):
            at = 2 * r + section
            tiles = in_ref[section * rows + r]
            wide_ref[16 * at : 16 * at + 16, :] = tiles[:2].astype(F32).reshape(16, count)
            if at < 8:
                few_ref[8 * at : 8 * at + 8, :] = tiles[2].astype(F32)
    zero_owns = jnp.where(lax.axis_index("section") == 0, owns_ref[...], 1.0 - owns_ref[...]) > 0.5
    results = triangles(wide_ref, few_ref, 8, place_ref, count)
    for c, (full, short) in enumerate(results):
        full = full.reshape(rows, 8, count)
        short = short.reshape(-1, 8, count)
        groups = short.shape[0]
        for section in range(2):
            is_full = zero_owns if section == 0 else jnp.logical_not(zero_owns)
            at = section * rows
            out_ref[at : at + groups, c] = jnp.where(is_full[None], full[:groups], short).astype(BF16)
            out_ref[at + groups : at + rows, c] = jnp.where(
                is_full[None], full[groups:], 0.0
            ).astype(BF16)


def picker(block, own_ref, other_ref):
    mine = lax.axis_index("section") == block

    def pick(start, size):
        here = slice(start, start + size)
        return jnp.where(mine, own_ref[here, :], other_ref[here, :])

    return pick


def gates_and_sides(block, inner, n_ref, own_ref, other_ref, gate_ref, w_out_ref, turned_ref=None):
    width = n_ref.shape[1]
    pick = picker(block, own_ref, other_ref)
    weights = pick(2 * width, width)
    step = 512
    for m in range(n_ref.shape[0] // step):
        here = slice(m * step, (m + 1) * step)
        gate_ref[here, :] = jax.nn.sigmoid(
            jnp.dot(n_ref[here, :], weights, preferred_element_type=F32)
        )
    w_out_ref[...] = pick(3 * width, inner)
    if turned_ref is not None:
        pick = picker(block + 1, own_ref, other_ref)
        sides = [pick(j * width, width) for j in range(2)]
        turned_ref[...] = tile_weights(jnp.concatenate(sides, -1), inner)


def transition_weights(block, own_ref, other_ref, in_ref, back_ref):
    width, hidden = in_ref.shape
    pick = picker(block, own_ref, other_ref)
    for j in range(hidden // width):
        in_ref[:, j * width : (j + 1) * width] = pick(j * width, width)
    back_ref[...] = pick(hidden, back_ref.shape[0])


def ready_last_kernel(
    inner, n_ref, own_ref, other_ref, large_ref, other_large_ref, gate_ref, w_out_ref, in_ref, back_ref
):
    gates_and_sides(1, inner, n_ref, own_ref, other_ref, gate_ref, w_out_ref)
    transition_weights(1, large_ref, other_large_ref, in_ref, back_ref)


def rows_norm(z_ref, n_ref):
    rows, count, _ = z_ref.shape
    for r in range(rows):
        n_ref[r * count : (r + 1) * count, :] = row_norm(z_ref[r])


def join_kernel(keep_ref, other_ref, z_ref, n_ref):
    half = keep_ref.shape[0]
    first = lax.axis_index("section") == 0
    z_ref[:half] = jnp.where(first, keep_ref[...], other_ref[...])
    z_ref[half:] = jnp.where(first, other_ref[...], keep_ref[...])
    rows_norm(z_ref, n_ref)


def out_project(which, t_ref, offsets, stride, z_ref, gate_ref, w_out, z1_ref, n_ref):
    _, count, _ = z_ref.shape
    inner = w_out.shape[0]
    for r in which:
        here = slice(r * count, (r + 1) * count)
        tri = t_ref[pl.ds(offsets[r], inner, stride=stride), :].astype(BF16)
        update = contract(tri, w_out, 0, 0)
        first = (z_ref[r].astype(F32) + gate_ref[here, :] * update).astype(BF16)
        z1_ref[here, :] = first
        n_ref[here, :] = row_norm(first)


def transition(which, in_ref, back_ref, n_ref, z1_ref, finish):
    trans, piece = back_ref.shape[0], 256
    for m in which:
        here = slice(m * STEP, (m + 1) * STEP)
        normed = n_ref[here, :]
        acts = []
        for j in range(trans // piece):
            gate_w = in_ref[:, j * piece : (j + 1) * piece]
            up_w = in_ref[:, trans + j * piece : trans + (j + 1) * piece]
            gate = jnp.dot(normed, gate_w, preferred_element_type=F32)
            up = jnp.dot(normed, up_w, preferred_element_type=F32)
            acts.append((jax.nn.silu(gate) * up).astype(BF16))
        back = jnp.dot(jnp.concatenate(acts, -1), back_ref[...], preferred_element_type=F32)
        finish(m, (z1_ref[here, :].astype(F32) + back).astype(BF16))


def norm_kernel(inner, tri_ref, t_ref):
    count = t_ref.shape[1]
    for q in range(2):
        part = tri_ref[:, q].astype(F32)

        def mean(value):
            total = jnp.sum(value, 0)
            return (total + pltpu.roll(total, 4, 0)) * (1.0 / inner)

        centred = part - mean(part)[None]
        var = mean(centred * centred)
        normed = centred * lax.rsqrt(var + 1e-05)[None]
        t_ref[q * 4 * inner : (q + 1) * 4 * inner, :] = normed.reshape(4 * inner, count)


def update_kernel(
    inner,
    t_ref,
    z_ref,
    gate_ref,
    w_out_ref,
    turned_ref,
    large_ref,
    other_large_ref,
    masks_ref,
    owns_ref,
    lr_ref,
    keep_ref,
    send_ref,
    n_ref,
    z1_ref,
    o_ref,
    in_ref,
    back_ref,
):
    rows, count, width = z_ref.shape
    half = rows // 2
    transition_weights(0, large_ref, other_large_ref, in_ref, back_ref)
    offsets = [q * 4 * inner + r for q in range(2) for r in range(half)]
    project = functools.partial(
        out_project,
        t_ref=t_ref,
        offsets=offsets,
        stride=4,
        z_ref=z_ref,
        gate_ref=gate_ref,
        w_out=w_out_ref[...],
        z1_ref=z1_ref,
        n_ref=n_ref,
    )

    def finish(m, done):
        o_ref[m * STEP : (m + 1) * STEP, :] = done

    turned = turned_ref[...]

    def tail_full():
        normed = [row_norm(o_ref[r * count : (r + 1) * count, :]) for r in range(half)]
        put_tiles(
            turned, [normed[:2], normed[2:]], [masks_ref[0], masks_ref[1]], lr_ref, 0, inner
        )

    project(range(rows))
    transition((0, 1), in_ref, back_ref, n_ref, z1_ref, finish)
    tail_full()
    owns = (owns_ref[:1, :] > 0.5)[None]
    full = o_ref[: half * count, :].reshape(half, count, width)
    short = o_ref[half * count :, :].reshape(half, count, width)
    keep_ref[...] = jnp.where(owns, full.astype(F32), short.astype(F32)).astype(BF16)
    send_ref[...] = jnp.where(owns, short.astype(F32), full.astype(F32)).astype(BF16)
    four = row_norm(
        jnp.concatenate(
            [o_ref[r * count : r * count + SHORT, :] for r in range(half, rows)], 0
        )
    )
    put_tiles(turned, [[four, jnp.zeros_like(four)]], [masks_ref[2]], lr_ref, 2, inner)


def last_kernel(
    inner,
    tri_ref,
    z_ref,
    gate_ref,
    w_out_ref,
    in_ref,
    back_ref,
    out_ref,
    t_ref,
    n_ref,
    z1_ref,
    o_ref,
    sems,
):
    rows, count, width = z_ref.shape
    copies = []

    def finish(m, done):
        part = pl.ds(m * (STEP // count), STEP // count)
        o_ref[m * (STEP // count) : (m + 1) * (STEP // count)] = done.reshape(-1, count, width)
        copies.append(pltpu.make_async_copy(o_ref.at[part], out_ref.at[part], sems.at[m]))
        copies[-1].start()

    t_ref[...] = layer_norm(tri_ref[...].reshape(inner, rows, count).astype(F32), 0).reshape(
        inner * rows, count
    )
    args = (t_ref, range(rows), rows, z_ref, gate_ref, w_out_ref[...], z1_ref, n_ref)
    out_project(range(rows), *args)
    transition((0, 1), in_ref, back_ref, n_ref, z1_ref, finish)
    for copy in copies:
        copy.wait()


def fast_body(pair, valid_tokens, crop_order, w_proj, w_out, w_in, w_back):
    _, rows, count, width = pair.shape
    devices = lax.axis_size("section") * lax.axis_size("row")
    inner, trans = w_out.shape[1], w_back.shape[1]
    swap = [(0, 1), (1, 0)]

    vmem = pl.BlockSpec(memory_space=pltpu.VMEM)
    hbm = pl.BlockSpec(memory_space=pltpu.HBM)
    anywhere = pl.BlockSpec(memory_space=pl.ANY)
    shape = jax.ShapeDtypeStruct
    flat = pltpu.VMEM((rows * count, width), BF16)
    gates = shape((rows * count, width), F32)
    sems = pltpu.SemaphoreType.DMA

    def call(
        kernel, out_shape, n_in, scratch=(), out_specs=None, in_spec=vmem, cost=None, params=LIMIT
    ):
        many = isinstance(out_shape, tuple)
        specs = out_specs or ((vmem,) * len(out_shape) if many else vmem)
        return pl.pallas_call(
            kernel,
            out_shape=out_shape,
            in_specs=[in_spec] * n_in if isinstance(n_in, int) else n_in,
            out_specs=specs,
            scratch_shapes=list(scratch),
            compiler_params=params,
            cost_estimate=cost,
        )

    def exchange(value):
        return lax.all_to_all(value, ("section", "row"), split_axis=0, concat_axis=0, tiled=True)

    inputs = [
        pltpu.with_memory_space_constraint(x, pltpu.HBM)
        for x in (crop_order, valid_tokens, pair, w_proj, w_in, w_back, w_out)
    ]
    scalars = [
        pltpu.SMEM(crop_order.shape, jnp.int32),
        pltpu.SMEM(valid_tokens.shape, jnp.int32),
        pltpu.VMEM(pair.shape, BF16),
    ]
    tokens = shape((rows * count, width), BF16)
    lr_shape = (devices, rows // 2 + 1, 8, count)
    lr = call(
        functools.partial(first_kernel, inner),
        shape(lr_shape, BF16),
        4,
        [pltpu.VMEM(lr_shape, BF16)]
        + scalars
        + [pltpu.VMEM(w_proj.shape[1:], BF16), sems((5 + rows // 4,))],
        out_specs=hbm,
        in_spec=hbm,
    )(*inputs[:4])
    light = pl.CostEstimate(flops=34 * 10**6, bytes_accessed=10**6, transcendentals=2 * 10**5)
    small = call(
        small_kernel,
        shape((w_proj.shape[2] + inner, width), BF16),
        [hbm] * 2 + [anywhere],
        [sems((1 + w_proj.shape[2] // width,))],
        cost=light,
    )(inputs[3], inputs[6], lr)
    large, z, normed, owns, masks = call(
        stage_kernel,
        (
            shape((3 * trans, width), BF16),
            shape((rows, count, width), BF16),
            tokens,
            shape((8, count), F32),
            shape((3, 8, count), F32),
        ),
        [hbm] * 5 + [anywhere],
        scalars + [sems((4 + 2 * trans // width,))],
        cost=light,
    )(*inputs[:3], *inputs[4:6], small)

    sides = exchange(lr)
    other_small = lax.ppermute(small, "section", swap)
    other_large = lax.ppermute(large, "section", swap)
    gate, w_out_first, turned = call(
        functools.partial(gates_and_sides, 0, inner),
        (gates, shape(w_out.shape[1:], BF16), shape((8 * inner, 2 * width), BF16)),
        3,
        cost=light,
    )(normed, small, other_small)
    tri_scratch = [
        pltpu.VMEM((4 * count, count), F32),
        pltpu.VMEM((32, count), F32),
        pltpu.VMEM((CHANNELS, 32, count), F32),
    ]
    tri = exchange(
        call(
            first_triangle_kernel,
            shape((devices, 2, 8, count), BF16),
            [vmem, anywhere],
            tri_scratch,
        )(sides, gate),
    )
    t = call(functools.partial(norm_kernel, inner), shape((8 * inner, count), F32), 1)(tri)
    work = [pltpu.VMEM((8 * inner, count), F32), flat, flat]
    halves = shape((rows // 2, count, width), BF16)
    lr, keep, send = call(
        functools.partial(update_kernel, inner),
        (shape((devices, 3, 8, count), BF16), halves, halves),
        9,
        [flat] * 3 + [pltpu.VMEM(w_in.shape[1:], BF16), pltpu.VMEM(w_back.shape[1:], BF16)],
    )(t, z, gate, w_out_first, turned, large, other_large, masks, owns)

    sides = exchange(lr)
    came = lax.ppermute(send, "section", swap)
    z, normed = call(join_kernel, (shape((rows, count, width), BF16), tokens), 2)(keep, came)
    ready = call(
        functools.partial(ready_last_kernel, inner),
        tuple(shape(x, BF16 if i else F32) for i, x in enumerate(
            ((rows * count, width), w_out.shape[1:], w_in.shape[1:], w_back.shape[1:])
        )),
        5,
        cost=light,
    )(normed, small, other_small, large, other_large)
    tri_scratch[1] = pltpu.VMEM((64, count), F32)
    tri = exchange(
        call(
            last_triangle_kernel, shape((devices, CHANNELS, 8, count), BF16), 2, tri_scratch
        )(sides, owns),
    )
    out = call(
        functools.partial(last_kernel, inner),
        shape((rows, count, width), BF16),
        6,
        work + [pltpu.VMEM((rows, count, width), BF16), sems((rows * count // STEP,))],
        out_specs=hbm,
    )(tri, z, *ready)
    return out[None]


def pair_block(state, valid, row_start, w_proj, w_out, w_in, w_back):
    rows_here, count, width = state.shape
    inner, trans = w_out.shape[0], w_back.shape[0]
    normed = layer_norm(state.astype(F32)).astype(BF16).reshape(rows_here * count, width)
    proj = jnp.dot(normed, w_proj, preferred_element_type=F32).reshape(rows_here, count, -1)
    keep_cols = (jnp.arange(count) < valid).astype(F32)
    keep_rows = (row_start + jnp.arange(rows_here) < valid).astype(F32)
    mask = keep_rows[:, None, None] * keep_cols[None, :, None]
    left = (mask * jax.nn.sigmoid(proj[..., inner : 2 * inner]) * proj[..., :inner]).astype(BF16)
    right = (
        mask * jax.nn.sigmoid(proj[..., 3 * inner : 4 * inner]) * proj[..., 2 * inner : 3 * inner]
    ).astype(BF16)
    gate = jax.nn.sigmoid(proj[..., 4 * inner :])
    left_whole = lax.all_to_all(left, "row", split_axis=2, concat_axis=0, tiled=True)
    right_whole = lax.all_to_all(right, "row", split_axis=2, concat_axis=0, tiled=True)
    tri_part = jnp.einsum("ikc,jkc->ijc", left_whole, right_whole, preferred_element_type=F32)
    tri = lax.all_to_all(
        tri_part.astype(BF16), "row", split_axis=0, concat_axis=2, tiled=True
    ).astype(F32)
    tri_normed = layer_norm(tri).astype(BF16).reshape(rows_here * count, inner)
    update = jnp.dot(tri_normed, w_out, preferred_element_type=F32).reshape(rows_here, count, width)
    first = (state.astype(F32) + gate * update).astype(BF16)
    second = layer_norm(first.astype(F32)).astype(BF16).reshape(rows_here * count, width)
    hidden = jnp.dot(second, w_in, preferred_element_type=F32)
    act = (jax.nn.silu(hidden[:, :trans]) * hidden[:, trans:]).astype(BF16)
    back = jnp.dot(act, w_back, preferred_element_type=F32).reshape(rows_here, count, width)
    return (first.astype(F32) + back).astype(BF16)


def general_body(pair, valid_tokens, crop_order, w_proj, w_out, w_in, w_back):
    crops, rows_here = pair.shape[:2]
    row_start = lax.axis_index("row") * rows_here
    share = crops // lax.axis_size("section")
    section = lax.axis_index("section")
    weights = [
        lax.all_gather(w, "section", axis=0, tiled=True) for w in (w_proj, w_out, w_in, w_back)
    ]
    blocks = weights[0].shape[0]

    def one_crop(index, outputs):
        crop = crop_order[section * share + index]
        valid = valid_tokens[crop]
        state = lax.dynamic_index_in_dim(pair, crop, 0, keepdims=False)

        def apply_block(block, value):
            return pair_block(value, valid, row_start, *[w[block] for w in weights])

        final = lax.fori_loop(0, blocks, apply_block, state)
        return lax.dynamic_update_index_in_dim(outputs, final, index, 0)

    empty = jnp.zeros((share,) + pair.shape[1:], BF16)
    return lax.fori_loop(0, share, one_crop, empty)


def solution(mesh):
    sections, peers = mesh.shape["section"], mesh.shape["row"]

    def body(pair, valid_tokens, crop_order, w_proj, w_out, w_in, w_back):
        crops, rows, count, width = pair.shape
        inner, trans = w_out.shape[1], w_back.shape[1]
        fits = (
            sections == 2
            and crops == sections
            and w_proj.shape[0] == 1
            and rows == 8
            and count == width == 4 * SHORT
            and peers * rows == count
            and inner == 2 * CHANNELS * peers
            and w_proj.shape[2] == 3 * width
            and trans % 256 == 0
        )
        run = fast_body if fits else general_body
        return run(pair, valid_tokens, crop_order, w_proj, w_out, w_in, w_back)

    weights = P("section", None, None)
    return jax.shard_map(
        body,
        mesh=mesh,
        in_specs=(P(None, "row", None, None), P(), P(), weights, weights, weights, weights),
        out_specs=P("section", "row", None, None),
        check_vma=False,
    )
```

```python
import functools

import jax
import jax.numpy as jnp
from jax import lax
from jax.experimental import pallas as pl
from jax.experimental.pallas import tpu as pltpu
from jax.sharding import PartitionSpec as P


F32 = jnp.float32
BF16 = jnp.bfloat16
STEP = 512
CHANNELS = 2
SHORT = 32
LIMIT = pltpu.CompilerParams(vmem_limit_bytes=16 * 2**20)


def layer_norm(value, axis=-1):
    mean = jnp.mean(value, axis, keepdims=True)
    centred = value - mean
    var = jnp.mean(centred * centred, axis, keepdims=True)
    return centred * lax.rsqrt(var + 1e-05)


def row_norm(value):
    return layer_norm(value.astype(F32)).astype(BF16)


def contract(left, right, left_axis, right_axis):
    return lax.dot_general(
        left, right, (((left_axis,), (right_axis,)), ((), ())), preferred_element_type=F32
    )


def tile_weights(weights, inner):
    row = lax.broadcasted_iota(jnp.int32, (4 * inner, 2 * inner), 0)
    column = lax.broadcasted_iota(jnp.int32, (4 * inner, 2 * inner), 1)
    peer, slot = lax.div(row, 8), lax.rem(row, 4)
    source = lax.div(slot, 2) * inner + peer * CHANNELS + lax.rem(slot, 2)
    pick = jnp.where(column == source, 1.0, 0.0).astype(BF16)
    left, right = weights[:, : 2 * inner].astype(F32), weights[:, 2 * inner :].astype(F32)
    low = lax.broadcasted_iota(jnp.int32, left.shape, 1) < inner
    values = jnp.where(low, left, pltpu.roll(right, inner, 1)).astype(BF16)
    gates = jnp.where(low, pltpu.roll(left, inner, 1), right).astype(BF16)
    both = [contract(pick, part, 1, 1) for part in (values, gates)]
    half = lax.rem(lax.broadcasted_iota(jnp.int32, both[0].shape, 0), 8) < 4
    return jnp.concatenate(
        [
            jnp.concatenate([jnp.where(half, part, 0.0), jnp.where(half, 0.0, part)], -1)
            for part in both
        ],
        0,
    ).astype(BF16)


def put_tiles(turned, halves, masks, lr_ref, first, inner):
    peers, count = lr_ref.shape[0], lr_ref.shape[-1]
    normed = jnp.concatenate([jnp.concatenate(pair, -1) for pair in halves], 0)
    proj = contract(turned, normed, 1, 1)
    sides = jax.nn.sigmoid(proj[4 * inner :]) * proj[: 4 * inner]
    for i, mask in enumerate(masks):
        tile = sides[:, i * count : (i + 1) * count].reshape(peers, 8, count)
        lr_ref[:, first + i] = (tile * mask[None]).astype(BF16)


def full_mask(row, valid, count):
    half = lax.div(lax.broadcasted_iota(jnp.int32, (8, count), 0), 4)
    token = lax.broadcasted_iota(jnp.int32, (8, count), 1)
    return jnp.where(jnp.logical_and(row + half < valid, token < valid), 1.0, 0.0)


def short_mask(row, valid, count):
    half = lax.div(lax.broadcasted_iota(jnp.int32, (8, count), 0), 4)
    lane = lax.broadcasted_iota(jnp.int32, (8, count), 1)
    inside = row + 4 * half + lax.div(lane, SHORT) < valid
    return jnp.where(jnp.logical_and(inside, lax.rem(lane, SHORT) < valid), 1.0, 0.0)


def read_scalars(order_ref, valid_ref, order_s, valid_s, sems):
    copies = [
        pltpu.make_async_copy(order_ref, order_s, sems.at[0]),
        pltpu.make_async_copy(valid_ref, valid_s, sems.at[1]),
    ]
    for copy in copies:
        copy.start()
    return copies


def first_kernel(
    inner, order_ref, valid_ref, pair_ref, wp_ref, out_ref, lr_ref, order_s, valid_s, both_ref, w_ref, sems
):
    rows, count, width = pair_ref.shape[1:]
    copies = []

    def send(first, tiles):
        part = pl.ds(first, tiles)
        copies.append(
            pltpu.make_async_copy(lr_ref.at[:, part], out_ref.at[:, part], sems.at[4 + len(copies)])
        )
        copies[-1].start()

    @pl.when(lax.axis_index("section") == 0)
    def _():
        weights = pltpu.make_async_copy(wp_ref.at[0], w_ref, sems.at[2])
        weights.start()
        state = pltpu.make_async_copy(pair_ref, both_ref, sems.at[3])
        state.start()
        scalars = read_scalars(order_ref, valid_ref, order_s, valid_s, sems)
        for copy in scalars:
            copy.wait()
        full = jnp.where(valid_s[1] > valid_s[0], 1, 0)
        short = 1 - full
        start = lax.axis_index("row") * rows
        weights.wait()
        state.wait()
        turned = tile_weights(w_ref[:, : 4 * inner], inner)
        for t in range(0, rows // 2, 2):
            normed = [row_norm(both_ref[full, 2 * t + r]) for r in range(4)]
            put_tiles(
                turned,
                [normed[:2], normed[2:]],
                [full_mask(start + 2 * t + r, valid_s[full], count) for r in (0, 2)],
                lr_ref,
                t,
                inner,
            )
            send(t, 2)
        fours = [
            row_norm(both_ref[short, 4 * h : 4 * h + 4, :SHORT].reshape(4 * SHORT, width))
            for h in range(2)
        ]
        put_tiles(
            turned, [fours], [short_mask(start, valid_s[short], count)], lr_ref, rows // 2, inner
        )
        send(rows // 2, 1)
        for copy in copies:
            copy.wait()


def pack(sources, target_ref, sems, first):
    copies, at = [], 0
    for i, source in enumerate(sources):
        part = target_ref.at[pl.ds(at, source.shape[0])]
        copies.append(pltpu.make_async_copy(source, part, sems.at[first + i]))
        copies[-1].start()
        at += source.shape[0]
    return copies


def small_kernel(wp_ref, w_out_ref, after_ref, small_ref, sems):
    width = small_ref.shape[1]
    sources = [wp_ref.at[0, :, pl.ds(j * width, width)] for j in range(wp_ref.shape[2] // width)]
    for copy in pack(sources + [w_out_ref.at[0]], small_ref, sems, 0):
        copy.wait()


def stage_kernel(
    order_ref,
    valid_ref,
    pair_ref,
    w_in_ref,
    w_back_ref,
    after_ref,
    large_ref,
    z_ref,
    n_ref,
    owns_ref,
    masks_ref,
    order_s,
    valid_s,
    both_ref,
    sems,
):
    rows, count, width = z_ref.shape
    trans = w_back_ref.shape[1]
    sources = [w_in_ref.at[0, :, pl.ds(j * width, width)] for j in range(2 * trans // width)]
    packing = pack(sources + [w_back_ref.at[0]], large_ref, sems, 3)
    scalars = read_scalars(order_ref, valid_ref, order_s, valid_s, sems)
    state = pltpu.make_async_copy(pair_ref, both_ref, sems.at[2])
    state.start()
    for copy in scalars:
        copy.wait()
    section = lax.axis_index("section")
    full = jnp.where(valid_s[1] > valid_s[0], 1, 0)
    short = 1 - full
    owns_ref[...] = jnp.full(owns_ref.shape, jnp.where(order_s[section] == full, 1.0, 0.0))
    mine = lax.axis_index("row") * rows + (rows // 2) * section
    masks_ref[0] = full_mask(mine, valid_s[full], count)
    masks_ref[1] = full_mask(mine + 2, valid_s[full], count)
    masks_ref[2] = short_mask(mine, valid_s[short], count)
    state.wait()
    half = pl.ds((rows // 2) * section, rows // 2)
    z_ref[: rows // 2] = both_ref[full, half]
    z_ref[rows // 2 :] = both_ref[short, half]
    rows_norm(z_ref, n_ref)
    for copy in packing:
        copy.wait()


def short_triangle(left, right, place_ref):
    count = left.shape[1]
    block = lax.div(lax.broadcasted_iota(jnp.int32, left.shape, 1), SHORT)
    lefts = jnp.concatenate([jnp.where(block == q, left, 0.0) for q in range(4)], 0)
    turned = [right if q == 0 else pltpu.roll(right, SHORT * q, 1) for q in range(4)]
    rights = jnp.concatenate(turned * 4, 0)
    product = contract(lefts.astype(BF16), rights.astype(BF16), 1, 1)
    row = lax.div(lax.broadcasted_iota(jnp.int32, product.shape, 0), 8)
    group = lax.div(lax.broadcasted_iota(jnp.int32, product.shape, 1), SHORT)
    product = jnp.where(row == group, product, 0.0).astype(BF16)
    source = lax.broadcasted_iota(jnp.int32, (count, count), 0)
    target = lax.broadcasted_iota(jnp.int32, (count, count), 1)
    moved, token = lax.rem(lax.div(source, 8), 4), lax.rem(source, 8)
    lane = 4 * token + lax.rem(lax.div(source, SHORT) - moved + 4, 4)
    pick = jnp.where(target == lane, 1.0, 0.0).astype(BF16)
    placed = jnp.dot(product, pick, preferred_element_type=F32)
    for q in range(4):
        place_ref[pl.ds(q, 8, stride=4), :] = placed[8 * q : 8 * q + 8]


def triangles(wide_ref, few_ref, few_stride, place_ref, count):
    results = []
    for c in range(CHANNELS):
        left = wide_ref[pl.ds(c, count, stride=4), :].astype(BF16)
        right = wide_ref[pl.ds(2 + c, count, stride=4), :].astype(BF16)
        short_triangle(
            few_ref[pl.ds(c, 8, stride=few_stride), :],
            few_ref[pl.ds(2 + c, 8, stride=few_stride), :],
            place_ref.at[c],
        )
        results.append((contract(left, right, 1, 1), place_ref[c]))
    return results


def first_triangle_kernel(in_ref, after_ref, out_ref, wide_ref, few_ref, place_ref):
    peers, count = in_ref.shape[0], in_ref.shape[-1]
    rows = peers // 2
    tiles = in_ref.shape[1] - 1
    wide_ref[...] = in_ref[:rows, :tiles].astype(F32).reshape(rows * tiles * 8, count)
    few_ref[...] = in_ref[:4, tiles].astype(F32).reshape(32, count)
    results = triangles(wide_ref, few_ref, 4, place_ref, count)
    for q in range(2):
        one, two = [r[q].reshape(-1, 8, count) for r in results]
        low = lax.broadcasted_iota(jnp.int32, one.shape, 1) < 4
        groups = one.shape[0]
        tiles = (
            jnp.where(low, one, pltpu.roll(two, 4, 1)),
            jnp.where(low, pltpu.roll(one, 4, 1), two),
        )
        for section, tile in enumerate(tiles):
            out_ref[section * rows : section * rows + groups, q] = tile.astype(BF16)
            if groups < rows:
                out_ref[section * rows + groups : (section + 1) * rows, q] = jnp.zeros(
                    (rows - groups, 8, count), BF16
                )


def last_triangle_kernel(in_ref, owns_ref, out_ref, wide_ref, few_ref, place_ref):
    peers, count = in_ref.shape[0], in_ref.shape[-1]
    rows = peers // 2
    for r in range(rows):
        for section in range(2):
            at = 2 * r + section
            tiles = in_ref[section * rows + r]
            wide_ref[16 * at : 16 * at + 16, :] = tiles[:2].astype(F32).reshape(16, count)
            if at < 8:
                few_ref[8 * at : 8 * at + 8, :] = tiles[2].astype(F32)
    zero_owns = jnp.where(lax.axis_index("section") == 0, owns_ref[...], 1.0 - owns_ref[...]) > 0.5
    results = triangles(wide_ref, few_ref, 8, place_ref, count)
    for c, (full, short) in enumerate(results):
        full = full.reshape(rows, 8, count)
        short = short.reshape(-1, 8, count)
        groups = short.shape[0]
        for section in range(2):
            is_full = zero_owns if section == 0 else jnp.logical_not(zero_owns)
            at = section * rows
            out_ref[at : at + groups, c] = jnp.where(is_full[None], full[:groups], short).astype(BF16)
            out_ref[at + groups : at + rows, c] = jnp.where(
                is_full[None], full[groups:], 0.0
            ).astype(BF16)


def picker(block, own_ref, other_ref):
    mine = lax.axis_index("section") == block

    def pick(start, size):
        here = slice(start, start + size)
        return jnp.where(mine, own_ref[here, :], other_ref[here, :])

    return pick


def gates_and_sides(block, inner, n_ref, own_ref, other_ref, gate_ref, w_out_ref, turned_ref=None):
    width = n_ref.shape[1]
    pick = picker(block, own_ref, other_ref)
    weights = pick(2 * width, width)
    step = 512
    for m in range(n_ref.shape[0] // step):
        here = slice(m * step, (m + 1) * step)
        gate_ref[here, :] = jax.nn.sigmoid(
            jnp.dot(n_ref[here, :], weights, preferred_element_type=F32)
        )
    w_out_ref[...] = pick(3 * width, inner)
    if turned_ref is not None:
        pick = picker(block + 1, own_ref, other_ref)
        sides = [pick(j * width, width) for j in range(2)]
        turned_ref[...] = tile_weights(jnp.concatenate(sides, -1), inner)


def transition_weights(block, own_ref, other_ref, in_ref, back_ref):
    width, hidden = in_ref.shape
    pick = picker(block, own_ref, other_ref)
    for j in range(hidden // width):
        in_ref[:, j * width : (j + 1) * width] = pick(j * width, width)
    back_ref[...] = pick(hidden, back_ref.shape[0])


def ready_last_kernel(
    inner, n_ref, own_ref, other_ref, large_ref, other_large_ref, gate_ref, w_out_ref, in_ref, back_ref
):
    gates_and_sides(1, inner, n_ref, own_ref, other_ref, gate_ref, w_out_ref)
    transition_weights(1, large_ref, other_large_ref, in_ref, back_ref)


def rows_norm(z_ref, n_ref):
    rows, count, _ = z_ref.shape
    for r in range(rows):
        n_ref[r * count : (r + 1) * count, :] = row_norm(z_ref[r])


def split_kernel(o_ref, owns_ref, after_ref, keep_ref, send_ref):
    half, count, width = keep_ref.shape
    owns = (owns_ref[:1, :] > 0.5)[None]
    full = o_ref[: half * count, :].reshape(half, count, width)
    short = o_ref[half * count :, :].reshape(half, count, width)
    keep_ref[...] = jnp.where(owns, full.astype(F32), short.astype(F32)).astype(BF16)
    send_ref[...] = jnp.where(owns, short.astype(F32), full.astype(F32)).astype(BF16)


def join_kernel(keep_ref, other_ref, z_ref, n_ref):
    half = keep_ref.shape[0]
    first = lax.axis_index("section") == 0
    z_ref[:half] = jnp.where(first, keep_ref[...], other_ref[...])
    z_ref[half:] = jnp.where(first, other_ref[...], keep_ref[...])
    rows_norm(z_ref, n_ref)


def out_project(which, t_ref, offsets, stride, z_ref, gate_ref, w_out, z1_ref, n_ref):
    _, count, _ = z_ref.shape
    inner = w_out.shape[0]
    for r in which:
        here = slice(r * count, (r + 1) * count)
        tri = t_ref[pl.ds(offsets[r], inner, stride=stride), :].astype(BF16)
        update = contract(tri, w_out, 0, 0)
        first = (z_ref[r].astype(F32) + gate_ref[here, :] * update).astype(BF16)
        z1_ref[here, :] = first
        n_ref[here, :] = row_norm(first)


def transition(which, in_ref, back_ref, n_ref, z1_ref, finish):
    trans, piece = back_ref.shape[0], 256
    for m in which:
        here = slice(m * STEP, (m + 1) * STEP)
        normed = n_ref[here, :]
        acts = []
        for j in range(trans // piece):
            gate_w = in_ref[:, j * piece : (j + 1) * piece]
            up_w = in_ref[:, trans + j * piece : trans + (j + 1) * piece]
            gate = jnp.dot(normed, gate_w, preferred_element_type=F32)
            up = jnp.dot(normed, up_w, preferred_element_type=F32)
            acts.append((jax.nn.silu(gate) * up).astype(BF16))
        back = jnp.dot(jnp.concatenate(acts, -1), back_ref[...], preferred_element_type=F32)
        finish(m, (z1_ref[here, :].astype(F32) + back).astype(BF16))


def norm_kernel(inner, tri_ref, t_ref):
    count = t_ref.shape[1]
    for q in range(2):
        part = tri_ref[:, q].astype(F32)

        def mean(value):
            total = jnp.sum(value, 0)
            return (total + pltpu.roll(total, 4, 0)) * (1.0 / inner)

        centred = part - mean(part)[None]
        var = mean(centred * centred)
        normed = centred * lax.rsqrt(var + 1e-05)[None]
        t_ref[q * 4 * inner : (q + 1) * 4 * inner, :] = normed.reshape(4 * inner, count)


def update_kernel(
    inner,
    t_ref,
    z_ref,
    gate_ref,
    w_out_ref,
    turned_ref,
    large_ref,
    other_large_ref,
    masks_ref,
    lr_ref,
    o_ref,
    n_ref,
    z1_ref,
    in_ref,
    back_ref,
):
    rows, count, _ = z_ref.shape
    half = rows // 2
    transition_weights(0, large_ref, other_large_ref, in_ref, back_ref)
    offsets = [q * 4 * inner + r for q in range(2) for r in range(half)]
    project = functools.partial(
        out_project,
        t_ref=t_ref,
        offsets=offsets,
        stride=4,
        z_ref=z_ref,
        gate_ref=gate_ref,
        w_out=w_out_ref[...],
        z1_ref=z1_ref,
        n_ref=n_ref,
    )

    def finish(m, done):
        o_ref[m * STEP : (m + 1) * STEP, :] = done

    turned = turned_ref[...]

    def tail_full():
        normed = [row_norm(o_ref[r * count : (r + 1) * count, :]) for r in range(half)]
        put_tiles(
            turned, [normed[:2], normed[2:]], [masks_ref[0], masks_ref[1]], lr_ref, 0, inner
        )

    project(range(rows))
    transition((0, 1), in_ref, back_ref, n_ref, z1_ref, finish)
    tail_full()
    four = row_norm(
        jnp.concatenate(
            [o_ref[r * count : r * count + SHORT, :] for r in range(half, rows)], 0
        )
    )
    put_tiles(turned, [[four, jnp.zeros_like(four)]], [masks_ref[2]], lr_ref, 2, inner)


def last_kernel(
    inner,
    tri_ref,
    z_ref,
    gate_ref,
    w_out_ref,
    in_ref,
    back_ref,
    out_ref,
    t_ref,
    n_ref,
    z1_ref,
    o_ref,
    sems,
):
    rows, count, width = z_ref.shape
    copies = []

    def finish(m, done):
        part = pl.ds(m * (STEP // count), STEP // count)
        o_ref[m * (STEP // count) : (m + 1) * (STEP // count)] = done.reshape(-1, count, width)
        copies.append(pltpu.make_async_copy(o_ref.at[part], out_ref.at[part], sems.at[m]))
        copies[-1].start()

    t_ref[...] = layer_norm(tri_ref[...].reshape(inner, rows, count).astype(F32), 0).reshape(
        inner * rows, count
    )
    args = (t_ref, range(rows), rows, z_ref, gate_ref, w_out_ref[...], z1_ref, n_ref)
    out_project(range(rows), *args)
    transition((0, 1), in_ref, back_ref, n_ref, z1_ref, finish)
    for copy in copies:
        copy.wait()


def fast_body(pair, valid_tokens, crop_order, w_proj, w_out, w_in, w_back):
    _, rows, count, width = pair.shape
    devices = lax.axis_size("section") * lax.axis_size("row")
    inner, trans = w_out.shape[1], w_back.shape[1]
    swap = [(0, 1), (1, 0)]

    vmem = pl.BlockSpec(memory_space=pltpu.VMEM)
    hbm = pl.BlockSpec(memory_space=pltpu.HBM)
    anywhere = pl.BlockSpec(memory_space=pl.ANY)
    shape = jax.ShapeDtypeStruct
    flat = pltpu.VMEM((rows * count, width), BF16)
    gates = shape((rows * count, width), F32)
    sems = pltpu.SemaphoreType.DMA

    def call(
        kernel, out_shape, n_in, scratch=(), out_specs=None, in_spec=vmem, cost=None, params=LIMIT
    ):
        many = isinstance(out_shape, tuple)
        specs = out_specs or ((vmem,) * len(out_shape) if many else vmem)
        return pl.pallas_call(
            kernel,
            out_shape=out_shape,
            in_specs=[in_spec] * n_in if isinstance(n_in, int) else n_in,
            out_specs=specs,
            scratch_shapes=list(scratch),
            compiler_params=params,
            cost_estimate=cost,
        )

    def exchange(value):
        return lax.all_to_all(value, ("section", "row"), split_axis=0, concat_axis=0, tiled=True)

    inputs = [
        pltpu.with_memory_space_constraint(x, pltpu.HBM)
        for x in (crop_order, valid_tokens, pair, w_proj, w_in, w_back, w_out)
    ]
    scalars = [
        pltpu.SMEM(crop_order.shape, jnp.int32),
        pltpu.SMEM(valid_tokens.shape, jnp.int32),
        pltpu.VMEM(pair.shape, BF16),
    ]
    tokens = shape((rows * count, width), BF16)
    lr_shape = (devices, rows // 2 + 1, 8, count)
    lr = call(
        functools.partial(first_kernel, inner),
        shape(lr_shape, BF16),
        4,
        [pltpu.VMEM(lr_shape, BF16)]
        + scalars
        + [pltpu.VMEM(w_proj.shape[1:], BF16), sems((5 + rows // 4,))],
        out_specs=hbm,
        in_spec=hbm,
    )(*inputs[:4])
    light = pl.CostEstimate(flops=34 * 10**6, bytes_accessed=10**6, transcendentals=2 * 10**5)
    small = call(
        small_kernel,
        shape((w_proj.shape[2] + inner, width), BF16),
        [hbm] * 2 + [anywhere],
        [sems((1 + w_proj.shape[2] // width,))],
        cost=light,
    )(inputs[3], inputs[6], lr)
    large, z, normed, owns, masks = call(
        stage_kernel,
        (
            shape((3 * trans, width), BF16),
            shape((rows, count, width), BF16),
            tokens,
            shape((8, count), F32),
            shape((3, 8, count), F32),
        ),
        [hbm] * 5 + [anywhere],
        scalars + [sems((4 + 2 * trans // width,))],
        cost=light,
    )(*inputs[:3], *inputs[4:6], small)

    sides = exchange(lr)
    other_small = lax.ppermute(small, "section", swap)
    other_large = lax.ppermute(large, "section", swap)
    gate, w_out_first, turned = call(
        functools.partial(gates_and_sides, 0, inner),
        (gates, shape(w_out.shape[1:], BF16), shape((8 * inner, 2 * width), BF16)),
        3,
        cost=light,
    )(normed, small, other_small)
    tri_scratch = [
        pltpu.VMEM((4 * count, count), F32),
        pltpu.VMEM((32, count), F32),
        pltpu.VMEM((CHANNELS, 32, count), F32),
    ]
    tri = exchange(
        call(
            first_triangle_kernel,
            shape((devices, 2, 8, count), BF16),
            [vmem, anywhere],
            tri_scratch,
        )(sides, gate),
    )
    t = call(functools.partial(norm_kernel, inner), shape((8 * inner, count), F32), 1)(tri)
    work = [pltpu.VMEM((8 * inner, count), F32), flat, flat]
    halves = shape((rows // 2, count, width), BF16)
    lr, state = call(
        functools.partial(update_kernel, inner),
        (shape((devices, 3, 8, count), BF16), tokens),
        8,
        [flat] * 2 + [pltpu.VMEM(w_in.shape[1:], BF16), pltpu.VMEM(w_back.shape[1:], BF16)],
    )(t, z, gate, w_out_first, turned, large, other_large, masks)

    sides = exchange(lr)
    tri_scratch[1] = pltpu.VMEM((64, count), F32)
    part = call(
        last_triangle_kernel, shape((devices, CHANNELS, 8, count), BF16), 2, tri_scratch
    )(sides, owns)
    keep, send = call(split_kernel, (halves, halves), [vmem, vmem, anywhere], cost=light)(
        state, owns, part
    )
    came = lax.ppermute(send, "section", swap)
    z, normed = call(join_kernel, (shape((rows, count, width), BF16), tokens), 2)(keep, came)
    ready = call(
        functools.partial(ready_last_kernel, inner),
        tuple(shape(x, BF16 if i else F32) for i, x in enumerate(
            ((rows * count, width), w_out.shape[1:], w_in.shape[1:], w_back.shape[1:])
        )),
        5,
        cost=light,
    )(normed, small, other_small, large, other_large)
    tri = exchange(part)
    out = call(
        functools.partial(last_kernel, inner),
        shape((rows, count, width), BF16),
        6,
        work + [pltpu.VMEM((rows, count, width), BF16), sems((rows * count // STEP,))],
        out_specs=hbm,
    )(tri, z, *ready)
    return out[None]


def pair_block(state, valid, row_start, w_proj, w_out, w_in, w_back):
    rows_here, count, width = state.shape
    inner, trans = w_out.shape[0], w_back.shape[0]
    normed = layer_norm(state.astype(F32)).astype(BF16).reshape(rows_here * count, width)
    proj = jnp.dot(normed, w_proj, preferred_element_type=F32).reshape(rows_here, count, -1)
    keep_cols = (jnp.arange(count) < valid).astype(F32)
    keep_rows = (row_start + jnp.arange(rows_here) < valid).astype(F32)
    mask = keep_rows[:, None, None] * keep_cols[None, :, None]
    left = (mask * jax.nn.sigmoid(proj[..., inner : 2 * inner]) * proj[..., :inner]).astype(BF16)
    right = (
        mask * jax.nn.sigmoid(proj[..., 3 * inner : 4 * inner]) * proj[..., 2 * inner : 3 * inner]
    ).astype(BF16)
    gate = jax.nn.sigmoid(proj[..., 4 * inner :])
    left_whole = lax.all_to_all(left, "row", split_axis=2, concat_axis=0, tiled=True)
    right_whole = lax.all_to_all(right, "row", split_axis=2, concat_axis=0, tiled=True)
    tri_part = jnp.einsum("ikc,jkc->ijc", left_whole, right_whole, preferred_element_type=F32)
    tri = lax.all_to_all(
        tri_part.astype(BF16), "row", split_axis=0, concat_axis=2, tiled=True
    ).astype(F32)
    tri_normed = layer_norm(tri).astype(BF16).reshape(rows_here * count, inner)
    update = jnp.dot(tri_normed, w_out, preferred_element_type=F32).reshape(rows_here, count, width)
    first = (state.astype(F32) + gate * update).astype(BF16)
    second = layer_norm(first.astype(F32)).astype(BF16).reshape(rows_here * count, width)
    hidden = jnp.dot(second, w_in, preferred_element_type=F32)
    act = (jax.nn.silu(hidden[:, :trans]) * hidden[:, trans:]).astype(BF16)
    back = jnp.dot(act, w_back, preferred_element_type=F32).reshape(rows_here, count, width)
    return (first.astype(F32) + back).astype(BF16)


def general_body(pair, valid_tokens, crop_order, w_proj, w_out, w_in, w_back):
    crops, rows_here = pair.shape[:2]
    row_start = lax.axis_index("row") * rows_here
    share = crops // lax.axis_size("section")
    section = lax.axis_index("section")
    weights = [
        lax.all_gather(w, "section", axis=0, tiled=True) for w in (w_proj, w_out, w_in, w_back)
    ]
    blocks = weights[0].shape[0]

    def one_crop(index, outputs):
        crop = crop_order[section * share + index]
        valid = valid_tokens[crop]
        state = lax.dynamic_index_in_dim(pair, crop, 0, keepdims=False)

        def apply_block(block, value):
            return pair_block(value, valid, row_start, *[w[block] for w in weights])

        final = lax.fori_loop(0, blocks, apply_block, state)
        return lax.dynamic_update_index_in_dim(outputs, final, index, 0)

    empty = jnp.zeros((share,) + pair.shape[1:], BF16)
    return lax.fori_loop(0, share, one_crop, empty)


def solution(mesh):
    sections, peers = mesh.shape["section"], mesh.shape["row"]

    def body(pair, valid_tokens, crop_order, w_proj, w_out, w_in, w_back):
        crops, rows, count, width = pair.shape
        inner, trans = w_out.shape[1], w_back.shape[1]
        fits = (
            sections == 2
            and crops == sections
            and w_proj.shape[0] == 1
            and rows == 8
            and count == width == 4 * SHORT
            and peers * rows == count
            and inner == 2 * CHANNELS * peers
            and w_proj.shape[2] == 3 * width
            and trans % 256 == 0
        )
        run = fast_body if fits else general_body
        return run(pair, valid_tokens, crop_order, w_proj, w_out, w_in, w_back)

    weights = P("section", None, None)
    return jax.shard_map(
        body,
        mesh=mesh,
        in_specs=(P(None, "row", None, None), P(), P(), weights, weights, weights, weights),
        out_specs=P("section", "row", None, None),
        check_vma=False,
    )
```
